512 devices in a mesh: emb: 64 (over z, x), bal: 8 (over y, core).
Axes of the slice: x: 4, y: 4, z: 16, core: 2. Of those that a mesh axis runs over, the one named last changes fastest.
Arguments:
- item_ids: int32 [8, 16384, 16], P('bal'), may hold values from 0 to 1023
- seq_lengths: int32 [8, 64, 2], P(None, 'emb'), may hold values from 1 to 128, as said below
- surplus_slot: int32 [8, 64], P(None, 'emb'), may hold values from 0 to 1
- helper_map: int32 [8, 64], P(None, 'emb'), may hold values from 0 to 7, as said below
- embed_tables: bfloat16 [64, 1024, 128], P('emb'), may hold values from -1.5 to 1.5
- weight_in: bfloat16 [512, 2048], P('bal'), may hold values from -0.25 to 0.25
- weight_out: bfloat16 [512, 512], P('bal'), may hold values from -0.25 to 0.25
- cotangent: bfloat16 [8, 16384, 512], P('bal', 'emb'), may hold values from -6 to 6
Outputs:
- layer_out: bfloat16 [8, 16384, 512], P('bal', 'emb')
- table_grad: float32 [64, 1024, 128], P('emb', 'bal')
- grad_in: float32 [512, 2048], P('bal')
- grad_out: float32 [512, 512], P('bal')
The draws below stay inside these ranges and needn't reach their ends.
Inputs may be any that keep to these rules, and one draw needn't show every extreme that they name: `seq_lengths`: some slot has 128 live events. Each column helper_map[:, e] is a permutation of the bal indices.
All inputs are finite; a program needn't handle non-finite values.
Results may differ from the reference program's by a relative error of at most 0.014.
Values may be sent and summed in bfloat16 or wider, within the bound.
A program may use at most 64 MiB of HBM per device.

```python
import math
import jax
import jax.numpy as jnp
import numpy as np
from jax import lax

D = 512
HEADS = 8
F1 = 2048
COLS = 128
TABLES = 16
DISTINCT = 1024
SLOT = 128
NSEQ = 2
ROWS_DEV = 256
EMB_ROWS = 16384
EVENTS = 131072
N_EMB = 64
N_BAL = 8


def draw_seq_lengths(key, part):
    base_key = jax.random.fold_in(key, 101)
    first_key, second_key = jax.random.split(base_key)
    drawn = jax.random.randint(first_key, (N_BAL * N_EMB * NSEQ,), 0, SLOT, dtype=jnp.int32)
    lengths = 1 + drawn * drawn // SLOT
    position = jax.random.randint(second_key, (), 0, N_BAL * N_EMB * NSEQ, dtype=jnp.int32)
    lengths = lengths.at[position].set(SLOT)
    return lengths.reshape(N_BAL, N_EMB, NSEQ).astype(jnp.int32)


def draw_helper_map(key, part):
    base_key = jax.random.fold_in(key, 202)
    column_keys = jax.random.split(base_key, N_EMB)
    orders = jax.vmap(lambda column_key: jax.random.permutation(column_key, N_BAL))(column_keys)
    return jnp.transpose(orders).astype(jnp.int32)


def touch_ends(entries, rng, least, high):
    shape = entries.shape
    index_at = [jax.random.randint(jax.random.fold_in(rng, axis), (), 0, shape[axis]) for axis in range(len(shape))]
    entries = entries.at[tuple(index_at)].set(least)
    longest = shape.index(max(shape))
    index_at[longest] = (index_at[longest] + 1) % shape[longest]
    return entries.at[tuple(index_at)].set(high)


def block_scale(stream_key, dims, cuts, least, top_value):
    level, own = 1.0, jax.random.fold_in(stream_key, 6)
    for dim, parts in cuts:
        draws = jnp.exp(jax.random.uniform(jax.random.fold_in(own, dim), (parts,), jnp.float32, least / len(cuts), top_value / len(cuts)))
        level = level * jnp.repeat(draws, dims[dim] // parts).reshape([-1 if axis == dim else 1 for axis in range(len(dims))])
    return level


def rank_bounds(count, skew):
    portions = [(1 << 20) // math.isqrt(standing ** skew) + 1 for standing in range(1, count + 1)]
    spread = 1 + sum(portions) // (1 << 30)
    return np.cumsum(np.array([max(1, weight // spread) for weight in portions]))


def skewed_ids(rng, shape, amount, slope):
    grid = rank_bounds(amount, slope)
    lot = jax.random.randint(jax.random.fold_in(rng, 1), shape, 0, int(grid[amount - 1]))
    rank = jnp.searchsorted(jnp.asarray(grid, jnp.int32), lot, side="right")
    return jax.random.permutation(jax.random.fold_in(rng, 2), amount)[rank].astype(jnp.int32)


def bell_draw(key, shape, spread, reach, shards=(), held_as=jnp.bfloat16):
    loudness = block_scale(key, shape, shards, -0.22, 0.18) if shards else 1.0
    result = jax.random.normal(key, shape, jnp.float32) * spread * loudness
    return jnp.minimum(jnp.maximum(result, -reach), reach).astype(held_as)


def setup_inputs(seed: int = 0) -> dict:
    key_list = jax.random.split(jax.random.key(seed), 9)
    return {
        "item_ids": touch_ends(skewed_ids(key_list[0], (N_BAL, EMB_ROWS, TABLES), DISTINCT, 1), jax.random.fold_in(key_list[0], 3), 0, DISTINCT - 1).astype(jnp.int32),
        "seq_lengths": draw_seq_lengths(jax.random.fold_in(key_list[8], 71), 0),
        "surplus_slot": touch_ends(jax.random.randint(key_list[2], (N_BAL, N_EMB), 0, NSEQ), jax.random.fold_in(key_list[2], 1), 0, NSEQ - 1).astype(jnp.int32),
        "helper_map": draw_helper_map(jax.random.fold_in(key_list[8], 71), 0),
        "embed_tables": bell_draw(key_list[4], (N_EMB, DISTINCT, COLS), (TABLES ** -0.5), 1.5, ((0, 64),)),
        "weight_in": bell_draw(key_list[5], (D, F1), D ** -0.5, 0.25, ((0, 8),)),
        "weight_out": bell_draw(key_list[6], (D, D), D ** -0.5, 0.25, ((0, 8),)),
        "cotangent": bell_draw(key_list[7], (N_BAL, EMB_ROWS, D), 1.0, 6.0, ((0, 8), (1, 64))),
    }


EPS = 1e-05

def silu_grad(argument):
    logistic = jax.nn.sigmoid(argument)
    return logistic * (1.0 + argument * (1.0 - logistic))

def seq_mask(lengths, row_count, slot_rows):
    position = jnp.arange(row_count, dtype=jnp.int32)
    slot_of = position // slot_rows
    within = position - slot_of * slot_rows
    slot_ids = jnp.arange(lengths.shape[0], dtype=jnp.int32)
    row_length = lax.optimization_barrier(jnp.sum(jnp.where(slot_of[:, None] == slot_ids[None, :], lengths[None, :], 0), axis=1))
    same_slot = slot_of[:, None] == slot_of[None, :]
    causal = position[None, :] <= position[:, None]
    live = within[:, None] < row_length[:, None]
    return jnp.where(same_slot & causal & live, 1.0, 0.0).astype(jnp.float32)

def normalize(values):
    average = lax.optimization_barrier(jnp.mean(values, axis=1, keepdims=True))
    centred = values - average
    inverse = lax.rsqrt(lax.optimization_barrier(jnp.mean(centred * centred, axis=1, keepdims=True)) + EPS)
    return (centred * inverse, inverse)

def norm_back(incoming, normed, inverse):
    first = lax.optimization_barrier(jnp.mean(incoming, axis=1, keepdims=True))
    second = lax.optimization_barrier(jnp.mean(incoming * normed, axis=1, keepdims=True))
    return inverse * (incoming - first - normed * second)

def head_slices(heads_input, head_index, head_width, model_width):
    head_values = lax.dynamic_slice_in_dim(heads_input, head_index * head_width, head_width, 1)
    head_query = lax.dynamic_slice_in_dim(heads_input, model_width + head_index * head_width, head_width, 1)
    head_keys = lax.dynamic_slice_in_dim(heads_input, 2 * model_width + head_index * head_width, head_width, 1)
    return (head_values, head_query, head_keys)

def head_forward(heads_input, allowed, head_index, head_width, model_width, seq_bound):
    head_values, head_query, head_keys = head_slices(heads_input, head_index, head_width, model_width)
    scores = jnp.dot(head_query, head_keys.T, preferred_element_type=jnp.float32) * head_width ** (-0.5)
    silu_weights = (jax.nn.silu(scores) * allowed / seq_bound).astype(jnp.bfloat16)
    return jnp.dot(silu_weights, head_values, preferred_element_type=jnp.float32)

def head_backward(heads_input, allowed, grad_attended, head_index, head_width, model_width, seq_bound):
    head_values, head_query, head_keys = head_slices(heads_input, head_index, head_width, model_width)
    score_scale = head_width ** (-0.5)
    scores = jnp.dot(head_query, head_keys.T, preferred_element_type=jnp.float32) * score_scale
    silu_weights = (jax.nn.silu(scores) * allowed / seq_bound).astype(jnp.bfloat16)
    grad_head = lax.dynamic_slice_in_dim(grad_attended, head_index * head_width, head_width, 1)
    grad_weights = jnp.dot(grad_head, head_values.T, preferred_element_type=jnp.float32)
    grad_values = jnp.dot(silu_weights.T, grad_head, preferred_element_type=jnp.float32)
    grad_scores = (grad_weights * allowed / seq_bound * silu_grad(scores)).astype(jnp.bfloat16)
    grad_query = jnp.dot(grad_scores, head_keys, preferred_element_type=jnp.float32) * score_scale
    grad_keys = jnp.dot(grad_scores.T, head_query, preferred_element_type=jnp.float32) * score_scale
    return (grad_values, grad_query, grad_keys)

def join_heads(stacked):
    head_count, row_count, head_width = stacked.shape
    return jnp.transpose(stacked, (1, 0, 2)).reshape(row_count, head_count * head_width)

def layer_forward(inputs, lengths, weight_in, weight_out, head_count, slot_rows):
    row_count, model_width = inputs.shape
    head_width = model_width // head_count
    seq_bound = slot_rows
    allowed = seq_mask(lengths, row_count, slot_rows)
    normed_in, in_inverse = normalize(inputs.astype(jnp.float32))
    normed_half = normed_in.astype(jnp.bfloat16)
    projected = jnp.dot(normed_half, weight_in, preferred_element_type=jnp.float32)
    activated = jax.nn.silu(projected)
    gate_rows = activated[:, :model_width]
    heads_input = activated[:, model_width:].astype(jnp.bfloat16)
    head_ids = jnp.arange(head_count, dtype=jnp.int32)
    attended = lax.map(lambda head_index: head_forward(heads_input, allowed, head_index, head_width, model_width, seq_bound), head_ids)
    normed_out, out_inverse = normalize(join_heads(attended))
    mixed_rows = (normed_out * gate_rows).astype(jnp.bfloat16)
    forward_out = (inputs.astype(jnp.float32) + jnp.dot(mixed_rows, weight_out, preferred_element_type=jnp.float32)).astype(jnp.bfloat16)
    stored = (allowed, normed_in, in_inverse, normed_half, projected, gate_rows, heads_input, normed_out, out_inverse, mixed_rows)
    return (forward_out, stored)

def layer_backward(stored, cotangent, weight_in, weight_out, head_count, slot_rows):
    allowed, normed_in, in_inverse, normed_half, projected, gate_rows, heads_input, normed_out, out_inverse, mixed_rows = stored
    row_count, model_width = normed_in.shape
    head_width = model_width // head_count
    seq_bound = slot_rows
    partial_out = jnp.dot(mixed_rows.T, cotangent, preferred_element_type=jnp.float32)
    grad_mixed = jnp.dot(cotangent, weight_out.T, preferred_element_type=jnp.float32)
    grad_gate = grad_mixed * normed_out
    grad_attended = norm_back(grad_mixed * gate_rows, normed_out, out_inverse).astype(jnp.bfloat16)
    head_ids = jnp.arange(head_count, dtype=jnp.int32)
    head_grads = lax.map(lambda head_index: head_backward(heads_input, allowed, grad_attended, head_index, head_width, model_width, seq_bound), head_ids)
    grad_heads = jnp.concatenate([join_heads(head_grads[0]), join_heads(head_grads[1]), join_heads(head_grads[2])], axis=1)
    grad_projected = (jnp.concatenate([grad_gate, grad_heads], axis=1) * silu_grad(projected)).astype(jnp.bfloat16)
    partial_in = jnp.dot(normed_half.T, grad_projected, preferred_element_type=jnp.float32)
    grad_normed = jnp.dot(grad_projected, weight_in.T, preferred_element_type=jnp.float32)
    grad_rows = (cotangent.astype(jnp.float32) + norm_back(grad_normed, normed_in, in_inverse)).astype(jnp.bfloat16)
    return (grad_rows, partial_in, partial_out)

def reference(item_ids, seq_lengths, surplus_slot, helper_map, embed_tables, weight_in, weight_out, cotangent):
    group_count = D // COLS
    full_tables = jnp.transpose(embed_tables.reshape(TABLES, group_count, DISTINCT, COLS), (0, 2, 1, 3)).reshape(TABLES, DISTINCT, D)
    flat_ids = item_ids.reshape(-1, TABLES)
    summed = jnp.zeros((flat_ids.shape[0], D), jnp.float32)
    for table_index in range(TABLES):
        summed = summed + full_tables[table_index][flat_ids[:, table_index]].astype(jnp.float32)
    embedded = summed.astype(jnp.bfloat16).reshape(N_BAL, N_EMB, NSEQ, SLOT, D)
    bal_ids = jnp.arange(N_BAL, dtype=jnp.int32)
    emb_ids = jnp.arange(N_EMB, dtype=jnp.int32)[None, :]
    source = lax.optimization_barrier(jnp.sum(jnp.where(helper_map[:, None, :] == bal_ids[None, :, None], bal_ids[:, None, None], 0), axis=0)).astype(jnp.int32)
    source_slot = surplus_slot[source, emb_ids]
    arrived = embedded[source, emb_ids, source_slot]
    slot_ids = jnp.arange(NSEQ, dtype=jnp.int32)
    replaced = slot_ids[None, None, :] == surplus_slot[:, :, None]
    proc_rows = jnp.where(replaced[:, :, :, None, None], arrived[:, :, None], embedded)
    proc_lengths = jnp.where(replaced, seq_lengths[source, emb_ids, source_slot][:, :, None], seq_lengths)
    blocks = N_BAL * N_EMB
    input_blocks = proc_rows.reshape(blocks, ROWS_DEV, D)
    cot_blocks = cotangent.reshape(blocks, ROWS_DEV, D)
    length_blocks = proc_lengths.reshape(blocks, NSEQ)

    def accumulate(totals, pieces):
        rows_here, cot_here, lengths_here = pieces
        forward_out, stored = layer_forward(rows_here, lengths_here, weight_in, weight_out, HEADS, SLOT)
        grad_rows, partial_in, partial_out = layer_backward(stored, cot_here, weight_in, weight_out, HEADS, SLOT)
        rounded_in = lax.optimization_barrier(partial_in.astype(jnp.bfloat16)).astype(jnp.float32)
        rounded_out = lax.optimization_barrier(partial_out.astype(jnp.bfloat16)).astype(jnp.float32)
        return ((totals[0] + rounded_in, totals[1] + rounded_out), (forward_out, grad_rows))
    start = (jnp.zeros((D, 4 * D), jnp.float32), jnp.zeros((D, D), jnp.float32))
    totals, outputs = lax.scan(accumulate, start, (input_blocks, cot_blocks, length_blocks))
    layer_out = outputs[0].reshape(N_BAL, EMB_ROWS, D)
    grad_proc = outputs[1].reshape(N_BAL, N_EMB, NSEQ, SLOT, D)
    helper_slot = surplus_slot[helper_map, emb_ids]
    came_back = grad_proc[helper_map, emb_ids, helper_slot]
    anchor_grads = jnp.where(replaced[:, :, :, None, None], came_back[:, :, None], grad_proc).reshape(-1, D)
    table_list = []
    for table_index in range(TABLES):
        table_list.append(jnp.zeros((DISTINCT, D), jnp.float32).at[flat_ids[:, table_index]].add(anchor_grads.astype(jnp.float32)))
    stacked = jnp.stack(table_list)
    table_scale = (DISTINCT / (N_BAL * EMB_ROWS)) ** 0.5
    table_grad = jnp.transpose(stacked.reshape(TABLES, DISTINCT, group_count, COLS), (0, 2, 1, 3)).reshape(N_EMB, DISTINCT, COLS) * table_scale
    grad_scale = EVENTS ** (-0.5)
    return (layer_out, table_grad, totals[0] * grad_scale, totals[1] * grad_scale)
```

```python
import functools

import jax
import jax.numpy as jnp
from jax import lax
from jax.experimental import pallas as pl
from jax.experimental.pallas import tpu as pltpu
from jax.sharding import PartitionSpec as P

D = 512
HEADS = 8
COLS = 128
DISTINCT = 1024
SLOT = 128
NSEQ = 2
TABLES = 16
NZ = 16
NX = 4
NY = 4
NB = 8
EPS = 1e-05
BF = jnp.bfloat16
F32 = jnp.float32
VMEM_LIMIT = 64000 * 1024


def place():
    emb = lax.axis_index("emb")
    bal = lax.axis_index("bal")
    return emb // NX, emb % NX, bal // 2, bal % 2


def at(z, x, y, k):
    return {"emb": z * NX + x, "bal": y * 2 + k}


def rcopy(src, dst, send, recv, device):
    return pltpu.make_async_remote_copy(
        src_ref=src,
        dst_ref=dst,
        send_sem=send,
        recv_sem=recv,
        device_id=device,
        device_id_type=pl.DeviceIdType.MESH,
    )


def greet(devices):
    barrier = pltpu.get_barrier_semaphore()
    for device in devices:
        pl.semaphore_signal(barrier, inc=1, device_id=device, device_id_type=pl.DeviceIdType.MESH)
    pl.semaphore_wait(barrier, len(devices))


VM = pl.BlockSpec(memory_space=pltpu.VMEM)
ANY = pl.BlockSpec(memory_space=pl.ANY)
DMA = pltpu.SemaphoreType.DMA


Z_SLICES = [(d, s) for s in range(1, 9) for d in (-1, 1) if d < 0 or s < 8]
Z_INDEX = {pair: i for i, pair in enumerate(Z_SLICES)}


def gather_kernel(
    tab, win, wout, ids, meta, tabs, wfi, wfo, idall, metall,
    zs, zr, ys, yr, cs, cr, ws, wr, os_, or_, is_, ir, ms, mr, loc,
):
    z, x, y, k = place()
    right, left = at((z + 1) % NZ, x, y, k), at((z + NZ - 1) % NZ, x, y, k)
    yp, ym, y2 = (y + 1) % NY, (y + 3) % NY, (y + 2) % NY
    up, down = at(z, x, yp, k), at(z, x, ym, k)
    xp, xm, x2 = (x + 1) % NX, (x + 3) % NX, (x + 2) % NX
    east, west, far = at(z, xp, y, k), at(z, xm, y, k), at(z, x2, y, k)
    other = at(z, x, y, 1 - k)
    greet([right, left, up, down, east, west, far, other])

    sent = []

    def go(src, dst, send, recv, device):
        copy = rcopy(src, dst, send, recv, device)
        copy.start()
        sent.append(copy)

    def came(dst, send, recv, device):
        rcopy(dst, dst, send, recv, device).wait_recv()

    local = [
        pltpu.make_async_copy(tab, tabs.at[z], loc.at[0]),
        pltpu.make_async_copy(win.at[x], wfi.at[y, k, x], loc.at[1]),
        pltpu.make_async_copy(wout.at[x], wfo.at[y, k, x], loc.at[2]),
        pltpu.make_async_copy(ids, idall.at[y, k], loc.at[3]),
        pltpu.make_async_copy(meta, metall.at[x], loc.at[4]),
    ]
    go(tab.at[y, k], tabs.at[z, y, k], zs.at[0], zr.at[0], right)
    go(tab.at[y, k], tabs.at[z, y, k], zs.at[1], zr.at[1], left)
    for copy in local:
        copy.start()
    for i, (peer, dev) in enumerate(((xp, east), (xm, west), (x2, far))):
        go(meta, metall.at[x], ms.at[i], mr.at[i], dev)
    go(ids, idall.at[y, k], is_.at[0], ir.at[0], up)
    go(ids, idall.at[y, k], is_.at[1], ir.at[1], down)
    go(win.at[x], wfi.at[y, k, x], ws.at[0], wr.at[0], up)
    go(win.at[x], wfi.at[y, k, x], ws.at[1], wr.at[1], down)
    go(wout.at[x], wfo.at[y, k, x], os_.at[0], or_.at[0], up)
    go(wout.at[x], wfo.at[y, k, x], os_.at[1], or_.at[1], down)

    def slot(d, s):
        return (z + d * s + NZ) % NZ

    def weights_y_relay():
        came(idall.at[ym, k], is_.at[0], ir.at[0], up)
        go(idall.at[ym, k, 0:4], idall.at[ym, k, 0:4], is_.at[2], ir.at[2], up)
        came(idall.at[yp, k], is_.at[1], ir.at[1], down)
        go(idall.at[yp, k, 4:8], idall.at[yp, k, 4:8], is_.at[3], ir.at[3], down)
        for full, s_, r_, half in ((wfi, ws, wr, 1024), (wfo, os_, or_, 256)):
            came(full.at[ym, k, x], s_.at[0], r_.at[0], up)
            part = full.at[ym, k, x, :, 0:half]
            go(part, part, s_.at[2], r_.at[2], up)
            came(full.at[yp, k, x], s_.at[1], r_.at[1], down)
            part = full.at[yp, k, x, :, half:2 * half]
            go(part, part, s_.at[3], r_.at[3], down)

    def weights_x_send():
        came(idall.at[y2, k, 0:4], is_.at[2], ir.at[2], up)
        came(idall.at[y2, k, 4:8], is_.at[3], ir.at[3], down)
        local[3].wait()
        go(idall.at[:, k], idall.at[:, k], is_.at[4], ir.at[4], other)
        local[1].wait()
        local[2].wait()
        for full, s_, r_, half in ((wfi, ws, wr, 1024), (wfo, os_, or_, 256)):
            came(full.at[y2, k, x, :, 0:half], s_.at[2], r_.at[2], up)
            came(full.at[y2, k, x, :, half:2 * half], s_.at[3], r_.at[3], down)
            go(full.at[:, k, x], full.at[:, k, x], s_.at[4], r_.at[4], east)
            go(full.at[:, k, x], full.at[:, k, x], s_.at[5], r_.at[5], west)

    def weights_x_relay():
        for full, s_, r_ in ((wfi, ws, wr), (wfo, os_, or_)):
            came(full.at[:, k, xm], s_.at[4], r_.at[4], east)
            part = full.at[0:2, k, xm]
            go(part, part, s_.at[6], r_.at[6], east)
            came(full.at[:, k, xp], s_.at[5], r_.at[5], west)
            part = full.at[2:4, k, xp]
            go(part, part, s_.at[7], r_.at[7], west)

    def weights_core():
        for full, s_, r_ in ((wfi, ws, wr), (wfo, os_, or_)):
            came(full.at[0:2, k, x2], s_.at[6], r_.at[6], east)
            came(full.at[2:4, k, x2], s_.at[7], r_.at[7], west)
            go(full.at[:, k], full.at[:, k], s_.at[8], r_.at[8], other)

    for st in range(1, 11):
        for d in (-1, 1):
            if (d, st) not in Z_INDEX:
                continue
            i, zz = Z_INDEX[(d, st)], slot(d, st)
            mine = tabs.at[zz, y, k]
            onward = right if d < 0 else left
            came(mine, zs.at[i], zr.at[i], onward)
            if (d, st + 1) in Z_INDEX:
                j = Z_INDEX[(d, st + 1)]
                go(mine, mine, zs.at[j], zr.at[j], onward)
            go(mine, mine, ys.at[i, 0], yr.at[i, 0], up)
            go(mine, mine, ys.at[i, 1], yr.at[i, 1], down)
        for d in (-1, 1):
            if (d, st - 1) not in Z_INDEX:
                continue
            i, zz = Z_INDEX[(d, st - 1)], slot(d, st - 1)
            came(tabs.at[zz, ym, k], ys.at[i, 0], yr.at[i, 0], up)
            part = tabs.at[zz, ym, k, 0:64]
            go(part, part, ys.at[i, 2], yr.at[i, 2], up)
            came(tabs.at[zz, yp, k], ys.at[i, 1], yr.at[i, 1], down)
            part = tabs.at[zz, yp, k, 64:128]
            go(part, part, ys.at[i, 3], yr.at[i, 3], down)
        for d in (-1, 1):
            if (d, st - 2) not in Z_INDEX:
                continue
            i, zz = Z_INDEX[(d, st - 2)], slot(d, st - 2)
            came(tabs.at[zz, y2, k, 0:64], ys.at[i, 2], yr.at[i, 2], up)
            came(tabs.at[zz, y2, k, 64:128], ys.at[i, 3], yr.at[i, 3], down)
            go(tabs.at[zz, :, k], tabs.at[zz, :, k], cs.at[i], cr.at[i], other)
        if st == 1:
            weights_y_relay()
        if st == 2:
            weights_x_send()
        if st == 5:
            weights_x_relay()
        if st == 8:
            weights_core()

    for i, peer in enumerate((xm, xp, x2)):
        came(metall.at[peer], ms.at[i], mr.at[i], other)
    came(idall.at[:, 1 - k], is_.at[4], ir.at[4], other)
    came(wfi.at[:, 1 - k], ws.at[8], wr.at[8], other)
    came(wfo.at[:, 1 - k], os_.at[8], or_.at[8], other)
    for (d, s), i in Z_INDEX.items():
        came(tabs.at[slot(d, s), :, 1 - k], cs.at[i], cr.at[i], other)
    for copy in sent:
        copy.wait_send()
    local[0].wait()
    local[4].wait()


def gather_all(tab, win, wout, ids, meta):
    return pl.pallas_call(
        gather_kernel,
        name="gather_all",
        out_shape=(
            jax.ShapeDtypeStruct((NZ, NY, 2, 128, COLS), BF),
            jax.ShapeDtypeStruct((NY, 2, NX, 16, 2048), BF),
            jax.ShapeDtypeStruct((NY, 2, NX, 16, 512), BF),
            jax.ShapeDtypeStruct((NY, 2, 8, TABLES, SLOT), jnp.int32),
            jax.ShapeDtypeStruct((NX, 8, 128), jnp.int32),
        ),
        in_specs=[VM] * 5,
        out_specs=(ANY,) * 5,
        scratch_shapes=[
            DMA((15,)), DMA((15,)), DMA((15, 4)), DMA((15, 4)), DMA((15,)), DMA((15,)),
            DMA((9,)), DMA((9,)), DMA((9,)), DMA((9,)), DMA((5,)), DMA((5,)),
            DMA((3,)), DMA((3,)), DMA((5,)),
        ],
        compiler_params=pltpu.CompilerParams(collective_id=0, has_side_effects=True),
    )(tab, win, wout, ids, meta)


def lookup_kernel(sel, *refs):
    slots, (table, out, columns, total) = refs[:8], refs[8:]
    t = pl.program_id(0)

    @pl.when(t == 0)
    def _():
        for i in range(8):
            columns[i * SLOT:(i + 1) * SLOT, :] = jnp.transpose(slots[i][0])
        total[...] = jnp.zeros_like(total)

    lane = lax.broadcasted_iota(jnp.int32, (8 * SLOT, TABLES), 1)
    picked = jnp.sum(jnp.where(lane == t, columns[...], 0), axis=1, keepdims=True)
    acc = total[...]
    for part in range(4):
        vocab = lax.broadcasted_iota(jnp.int32, (8 * SLOT, 256), 1) + part * 256
        hot = jnp.where(picked == vocab, 1.0, 0.0).astype(BF)
        acc = acc + jnp.dot(
            hot, table[0, part * 256:(part + 1) * 256, :], preferred_element_type=F32
        )
    total[...] = acc

    @pl.when(t == TABLES - 1)
    def _():
        out[...] = acc.astype(BF)


def slot_spec(i):
    return pl.BlockSpec((1, TABLES, SLOT), lambda t, sel: (sel[i], 0, 0))


def lookup(sel, ids, tables):
    return pl.pallas_call(
        lookup_kernel,
        name="lookup",
        out_shape=jax.ShapeDtypeStruct((8 * SLOT, COLS), BF),
        grid_spec=pltpu.PrefetchScalarGridSpec(
            num_scalar_prefetch=1,
            grid=(TABLES,),
            in_specs=[slot_spec(i) for i in range(8)]
            + [pl.BlockSpec((1, DISTINCT, COLS), lambda t, sel: (t, 0, 0))],
            out_specs=pl.BlockSpec((8 * SLOT, COLS), lambda t, sel: (0, 0)),
            scratch_shapes=[
                pltpu.VMEM((8 * SLOT, TABLES), jnp.int32),
                pltpu.VMEM((8 * SLOT, COLS), F32),
            ],
        ),
    )(sel, *([ids] * 8), tables)


def scatter_kernel(sel, *refs):
    slots, (grads, out, rows) = refs[:8], refs[8:]
    t = pl.program_id(0)

    @pl.when(t == 0)
    def _():
        for i in range(8):
            rows[:, i * SLOT:(i + 1) * SLOT] = slots[i][0]

    picked = rows[pl.ds(t, 1), :]
    for part in range(4):
        vocab = lax.broadcasted_iota(jnp.int32, (256, 8 * SLOT), 0) + part * 256
        hot = jnp.where(picked == vocab, 1.0, 0.0).astype(BF)
        out[0, part * 256:(part + 1) * 256, :] = jnp.dot(
            hot, grads[...], preferred_element_type=F32
        ).astype(BF)


def scatter(sel, ids, grads):
    return pl.pallas_call(
        scatter_kernel,
        name="scatter",
        out_shape=jax.ShapeDtypeStruct((TABLES, DISTINCT, COLS), BF),
        grid_spec=pltpu.PrefetchScalarGridSpec(
            num_scalar_prefetch=1,
            grid=(TABLES,),
            in_specs=[slot_spec(i) for i in range(8)]
            + [pl.BlockSpec((8 * SLOT, COLS), lambda t, sel: (0, 0))],
            out_specs=pl.BlockSpec((1, DISTINCT, COLS), lambda t, sel: (t, 0, 0)),
            scratch_shapes=[pltpu.VMEM((TABLES, 8 * SLOT), jnp.int32)],
        ),
    )(sel, *([ids] * 8), grads)


def exchange_kernel(forward, src, out, send, recv, loc):
    z, x, y, k = place()
    peers = [(x + 1) % NX, (x + 3) % NX, (x + 2) % NX]
    devices = [at(z, peer, y, k) for peer in peers]
    greet(devices)

    def piece(ref, i, split):
        if split:
            return ref.at[:, pl.ds(pl.multiple_of(i * COLS, COLS), COLS)]
        return ref.at[i]

    copies = []
    for i, (peer, device) in enumerate(zip(peers, devices)):
        copy = rcopy(
            piece(src, peer, not forward), piece(out, x, forward), send.at[i], recv.at[i], device
        )
        copy.start()
        copies.append(copy)
    own = pltpu.make_async_copy(piece(src, x, not forward), piece(out, x, forward), loc)
    own.start()
    for i, source in enumerate((peers[1], peers[0], peers[2])):
        landed = piece(out, source, forward)
        rcopy(landed, landed, send.at[i], recv.at[i], devices[i]).wait_recv()
    for copy in copies:
        copy.wait_send()
    own.wait()


def exchange(array, forward):
    shape = (256, D) if forward else (NX, 256, COLS)
    return pl.pallas_call(
        functools.partial(exchange_kernel, forward),
        name="exchange_rows" if forward else "exchange_grads",
        out_shape=jax.ShapeDtypeStruct(shape, BF),
        in_specs=[VM],
        out_specs=VM,
        scratch_shapes=[DMA((3,)), DMA((3,)), DMA],
        compiler_params=pltpu.CompilerParams(
            collective_id=1 if forward else 2, has_side_effects=True
        ),
    )(array)


def reduce_kernel(
    part, wg, tout, wout,
    t1, ta, tl1, tr1, tl2, tr2, tb, tz,
    w1, wa, wl1, wr1, wl2, wr2, wb, vl1, vr1, vl2, vr2, wc, wz, oz, wd, od, we,
    cs, cr, ys, yr, zs, zr, loc,
    wcs, wcr, wxs, wxr, wys, wyr, wzs, wzr, wgs, wgr, wes, wer,
):
    z, x, y, k = place()
    yp, ym, y2 = (y + 1) % NY, (y + 3) % NY, (y + 2) % NY
    xp, xm, x2 = (x + 1) % NX, (x + 3) % NX, (x + 2) % NX
    up, down = at(z, x, yp, k), at(z, x, ym, k)
    east, west, far = at(z, xp, y, k), at(z, xm, y, k), at(z, x2, y, k)
    other = at(z, x, y, 1 - k)
    ring = [(at((z + o) % NZ, x, y, k), (z + o) % NZ) for o in range(1, NZ)]
    greet([up, down, east, west, far, other] + [device for device, _ in ring])

    sent = []

    def go(src, dst, send, recv, device):
        copy = rcopy(src, dst, send, recv, device)
        copy.start()
        sent.append(copy)

    def came(dst, send, recv, device):
        rcopy(dst, dst, send, recv, device).wait_recv()

    def add(*values):
        total = values[0].astype(F32)
        for value in values[1:]:
            total = total + value.astype(F32)
        return total

    for c in range(4):
        go(part.at[:, c, :, 1 - k], t1.at[c], cs.at[c], cr.at[c], other)
        if c == 0:
            go(wg.at[:, 1 - k], w1, wcs, wcr, other)
    tload = pltpu.make_async_copy(part.at[:, :, :, k], ta, loc.at[0])
    tload.start()
    wload = pltpu.make_async_copy(wg.at[:, k], wa, loc.at[1])
    wload.start()

    def tables_core(c):
        came(t1.at[c], cs.at[c], cr.at[c], other)
        for i in range(4):
            ta[i, c] = add(ta[i, c], t1[c, i]).astype(BF)
        go(ta.at[:, c, y2, 0:64], tl1.at[c], ys.at[c, 0], yr.at[c, 0], up)
        go(ta.at[:, c, y2, 64:128], tr1.at[c], ys.at[c, 1], yr.at[c, 1], down)

    def tables_y(c):
        came(tl1.at[c], ys.at[c, 0], yr.at[c, 0], up)
        ta[:, c, yp, 0:64] = add(ta[:, c, yp, 0:64], tl1[c]).astype(BF)
        go(ta.at[:, c, yp], tl2.at[c], ys.at[c, 2], yr.at[c, 2], up)
        came(tr1.at[c], ys.at[c, 1], yr.at[c, 1], down)
        ta[:, c, ym, 64:128] = add(ta[:, c, ym, 64:128], tr1[c]).astype(BF)
        go(ta.at[:, c, ym], tr2.at[c], ys.at[c, 3], yr.at[c, 3], down)

    def tables_z(c):
        came(tl2.at[c], ys.at[c, 2], yr.at[c, 2], up)
        came(tr2.at[c], ys.at[c, 3], yr.at[c, 3], down)
        tb[c] = add(ta[:, c, y], tl2[c], tr2[c]).astype(BF)

    def tables_send(o):
        device, zz = ring[o - 1]
        go(tb.at[zz % 4, zz // 4], tz.at[o - 1], zs.at[o - 1], zr.at[o - 1], device)

    wload.wait()
    came(w1, wcs, wcr, other)
    for i in range(4):
        wa[i] = add(wa[i], w1[i]).astype(BF)
    go(wa.at[0:2, x2], wl1, wxs.at[0], wxr.at[0], east)
    go(wa.at[2:4, x2], wr1, wxs.at[1], wxr.at[1], west)
    tload.wait()
    tables_core(0)
    tables_core(1)
    came(wl1, wxs.at[0], wxr.at[0], east)
    wa[0:2, xp] = add(wa[0:2, xp], wl1[...]).astype(BF)
    go(wa.at[:, xp], wl2, wxs.at[2], wxr.at[2], east)
    came(wr1, wxs.at[1], wxr.at[1], west)
    wa[2:4, xm] = add(wa[2:4, xm], wr1[...]).astype(BF)
    go(wa.at[:, xm], wr2, wxs.at[3], wxr.at[3], west)
    tables_core(2)
    tables_core(3)
    tables_y(0)
    tables_y(1)
    came(wl2, wxs.at[2], wxr.at[2], east)
    came(wr2, wxs.at[3], wxr.at[3], west)
    wb[...] = add(wa[:, x], wl2[...], wr2[...]).astype(BF)
    go(wb.at[y2, :, 0:1280], vl1, wys.at[0], wyr.at[0], up)
    go(wb.at[y2, :, 1280:2560], vr1, wys.at[1], wyr.at[1], down)
    tables_y(2)
    tables_y(3)
    came(vl1, wys.at[0], wyr.at[0], up)
    wb[yp, :, 0:1280] = add(wb[yp, :, 0:1280], vl1[...]).astype(BF)
    go(wb.at[yp], vl2, wys.at[2], wyr.at[2], up)
    came(vr1, wys.at[1], wyr.at[1], down)
    wb[ym, :, 1280:2560] = add(wb[ym, :, 1280:2560], vr1[...]).astype(BF)
    go(wb.at[ym], vr2, wys.at[3], wyr.at[3], down)
    for c in range(4):
        tables_z(c)
    came(vl2, wys.at[2], wyr.at[2], up)
    came(vr2, wys.at[3], wyr.at[3], down)
    summed = add(wb[y], vl2[...], vr2[...]).astype(BF)
    for j in range(20):
        wc[j] = summed[:, j * 128:(j + 1) * 128]
    for o in (8, 7, 9, 6, 10, 5, 11, 4, 12, 3, 13, 2, 14, 1, 15):
        device, zz = ring[o - 1]
        go(wc.at[zz], wz.at[o - 1], wzs.at[o - 1, 0], wzr.at[o - 1, 0], device)
        go(wc.at[16 + zz // 4], oz.at[o - 1], wzs.at[o - 1, 1], wzr.at[o - 1, 1], device)
    for o in (8, 7, 9, 6, 10, 5, 11, 4, 12, 3, 13, 2, 14, 1, 15):
        tables_send(o)
    total_in = wc[z].astype(F32)
    total_out = wc[16 + z // 4].astype(F32)
    for o in range(1, NZ):
        came(wz.at[o - 1], wzs.at[o - 1, 0], wzr.at[o - 1, 0], other)
        came(oz.at[o - 1], wzs.at[o - 1, 1], wzr.at[o - 1, 1], other)
        total_in = total_in + wz[o - 1].astype(F32)
        total_out = total_out + oz[o - 1].astype(F32)
    wd[z] = total_in
    od[z] = total_out
    for o in (8, 7, 9, 6, 10, 5, 11, 4, 12, 3, 13, 2, 14, 1, 15):
        device, zz = ring[o - 1]
        go(wd.at[z], wd.at[z], wgs.at[o - 1, 0], wgr.at[o - 1, 0], device)
        go(od.at[z], od.at[z], wgs.at[o - 1, 1], wgr.at[o - 1, 1], device)
    for o in range(1, NZ):
        source = (z + NZ - o) % NZ
        came(wd.at[source], wgs.at[o - 1, 0], wgr.at[o - 1, 0], other)
        came(od.at[source], wgs.at[o - 1, 1], wgr.at[o - 1, 1], other)
    for j in range(16):
        we[:, j * 128:(j + 1) * 128] = wd[j]
    for c in range(4):
        we[:, 2048 + c * 128:2048 + (c + 1) * 128] = od[4 * c]
    for i, device in enumerate((east, west, far)):
        go(we, wout.at[x], wes.at[i], wer.at[i], device)
    own = pltpu.make_async_copy(we, wout.at[x], loc.at[2])
    own.start()
    total = tb[z % 4, z // 4].astype(F32)
    for o in range(1, NZ):
        came(tz.at[o - 1], zs.at[o - 1], zr.at[o - 1], other)
        total = total + tz[o - 1].astype(F32)
    tout[...] = total
    for i, source in enumerate((xm, xp, x2)):
        came(wout.at[source], wes.at[i], wer.at[i], other)
    own.wait()
    for copy in sent:
        copy.wait_send()


def reduce_all(part, wg):
    v = pltpu.VMEM
    return pl.pallas_call(
        reduce_kernel,
        name="reduce_all",
        out_shape=(
            jax.ShapeDtypeStruct((128, COLS), F32),
            jax.ShapeDtypeStruct((NX, 16, 2560), F32),
        ),
        in_specs=[ANY, ANY],
        out_specs=(VM, VM),
        scratch_shapes=[
            v((4, 4, NY, 128, COLS), BF), v((4, 4, NY, 128, COLS), BF),
            v((4, 4, 64, COLS), BF), v((4, 4, 64, COLS), BF),
            v((4, 4, 128, COLS), BF), v((4, 4, 128, COLS), BF),
            v((4, 4, 128, COLS), BF), v((15, 128, COLS), BF),
            v((NY, NX, 16, 2560), BF), v((NY, NX, 16, 2560), BF),
            v((2, 16, 2560), BF), v((2, 16, 2560), BF),
            v((4, 16, 2560), BF), v((4, 16, 2560), BF), v((4, 16, 2560), BF),
            v((16, 1280), BF), v((16, 1280), BF), v((16, 2560), BF), v((16, 2560), BF),
            v((20, 16, 128), BF), v((15, 16, 128), BF), v((15, 16, 128), BF),
            v((16, 16, 128), F32), v((16, 16, 128), F32), v((16, 2560), F32),
            DMA((4,)), DMA((4,)), DMA((4, 4)), DMA((4, 4)), DMA((15,)), DMA((15,)), DMA((3,)),
            DMA, DMA, DMA((4,)), DMA((4,)), DMA((4,)), DMA((4,)),
            DMA((15, 2)), DMA((15, 2)), DMA((15, 2)), DMA((15, 2)), DMA((3,)), DMA((3,)),
        ],
        compiler_params=pltpu.CompilerParams(
            collective_id=3, has_side_effects=True, vmem_limit_bytes=VMEM_LIMIT
        ),
    )(part, wg)


def silu_grad(argument):
    logistic = jax.nn.sigmoid(argument)
    return logistic * (1.0 + argument * (1.0 - logistic))


def normalize(values):
    average = jnp.mean(values, axis=1, keepdims=True)
    centred = values - average
    inverse = lax.rsqrt(jnp.mean(centred * centred, axis=1, keepdims=True) + EPS)
    return centred * inverse, inverse


def norm_back(incoming, normed, inverse):
    first = jnp.mean(incoming, axis=1, keepdims=True)
    second = jnp.mean(incoming * normed, axis=1, keepdims=True)
    return inverse * (incoming - first - normed * second)


def dot(a, b, ca, cb):
    return lax.dot_general(a, b, (((ca,), (cb,)), ((), ())), preferred_element_type=F32)


def layer_kernel(lengths, rows, cot, w_in, w_out, out, grad, pin, pout, act, proj, att, gh):
    width = D // HEADS
    scale = width ** (-0.5)
    values = rows[...].astype(F32)
    normed_in, in_inverse = normalize(values)
    half_in = normed_in.astype(BF)
    projected = dot(half_in, w_in[...], 1, 0)
    proj[...] = projected
    activated = jax.nn.silu(projected)
    gate = activated[:, :D]
    act[...] = activated[:, D:].astype(BF)
    place_i = lax.broadcasted_iota(jnp.int32, (SLOT, SLOT), 0)
    place_j = lax.broadcasted_iota(jnp.int32, (SLOT, SLOT), 1)
    masks = [(place_j <= place_i) & (place_i < lengths[s]) for s in range(NSEQ)]

    def heads(s, h):
        r = slice(s * SLOT, (s + 1) * SLOT)
        v = act[r, h * width:(h + 1) * width]
        q = act[r, D + h * width:D + (h + 1) * width]
        key = act[r, 2 * D + h * width:2 * D + (h + 1) * width]
        return r, v, q, key

    for s in range(NSEQ):
        for h in range(HEADS):
            r, v, q, key = heads(s, h)
            scores = dot(q, key, 1, 1) * scale
            weights = jnp.where(masks[s], jax.nn.silu(scores) * (1.0 / SLOT), 0.0).astype(BF)
            att[r, h * width:(h + 1) * width] = dot(weights, v, 1, 0)
    normed_out, out_inverse = normalize(att[...])
    mixed = (normed_out * gate).astype(BF)
    out[...] = (values + dot(mixed, w_out[...], 1, 0)).astype(BF)
    cotangent = cot[...]
    pout[...] = dot(mixed, cotangent, 0, 0).astype(BF)
    grad_mixed = dot(cotangent, w_out[...], 1, 1)
    att[...] = norm_back(grad_mixed * gate, normed_out, out_inverse)
    gh[:, :D] = (grad_mixed * normed_out * silu_grad(proj[:, :D])).astype(BF)
    for s in range(NSEQ):
        for h in range(HEADS):
            r, v, q, key = heads(s, h)
            g = att[r, h * width:(h + 1) * width].astype(BF)
            scores = dot(q, key, 1, 1) * scale
            logistic = jax.nn.sigmoid(scores)
            weights = jnp.where(masks[s], scores * logistic * (1.0 / SLOT), 0.0).astype(BF)
            slope = logistic * (1.0 + scores * (1.0 - logistic))
            gw = dot(g, v, 1, 1)
            gs = jnp.where(masks[s], gw * (1.0 / SLOT) * slope, 0.0).astype(BF)
            parts = (
                dot(weights, g, 0, 0), dot(gs, key, 1, 0) * scale, dot(gs, q, 0, 0) * scale
            )
            for p in range(3):
                c = slice(D + p * D + h * width, D + p * D + (h + 1) * width)
                gh[r, c] = (parts[p] * silu_grad(proj[r, c])).astype(BF)
    grad_projected = gh[...]
    pin[...] = dot(half_in, grad_projected, 0, 0).astype(BF)
    grad_normed = dot(grad_projected, w_in[...], 1, 1)
    grad[...] = (
        cotangent.astype(F32) + norm_back(grad_normed, normed_in, in_inverse)
    ).astype(BF)


def layer(lengths, rows, cot, w_in, w_out):
    v = pltpu.VMEM
    return pl.pallas_call(
        layer_kernel,
        name="layer",
        out_shape=(
            jax.ShapeDtypeStruct((256, D), BF),
            jax.ShapeDtypeStruct((256, D), BF),
            jax.ShapeDtypeStruct((D, 4 * D), BF),
            jax.ShapeDtypeStruct((D, D), BF),
        ),
        in_specs=[pl.BlockSpec(memory_space=pltpu.SMEM)] + [VM] * 4,
        out_specs=(VM,) * 4,
        scratch_shapes=[
            v((256, 3 * D), BF), v((256, 4 * D), F32), v((256, D), F32), v((256, 4 * D), BF),
        ],
        compiler_params=pltpu.CompilerParams(vmem_limit_bytes=VMEM_LIMIT),
    )(lengths, rows, cot, w_in, w_out)


def on_device(
    item_ids, seq_lengths, surplus_slot, helper_map, embed_tables, weight_in, weight_out, cotangent
):
    z, x, y, k = place()
    bal = lax.axis_index("bal")
    near = lax.dynamic_slice_in_dim(item_ids[0], z * 1024, 1024, 0)
    ids = jnp.transpose(near.reshape(8, SLOT, TABLES), (0, 2, 1))
    meta = jnp.concatenate(
        [seq_lengths.reshape(16), surplus_slot.reshape(8), helper_map.reshape(8)]
    )
    meta = jnp.broadcast_to(jnp.pad(meta, (0, 96))[None], (8, 128))
    tabs, w_in, w_out, id_all, meta_all = gather_all(
        embed_tables.reshape(NY, 2, 128, COLS),
        weight_in.reshape(NX, 16, 2048),
        weight_out.reshape(NX, 16, 512),
        ids,
        meta,
    )
    facts = meta_all[:, 0, :32]
    lengths = facts[:, :16].reshape(NX, NB, NSEQ)
    surplus = facts[:, 16:24]
    helper = facts[:, 24:32]
    bals = jnp.arange(NB, dtype=jnp.int32)[None]
    is_source = helper == bal
    source = jnp.sum(jnp.where(is_source, bals, 0), axis=1)
    source_slot = jnp.sum(jnp.where(is_source, surplus, 0), axis=1)
    my_slot = jnp.sum(jnp.where(bals == bal, surplus, 0), axis=1)
    slots = jnp.arange(NSEQ, dtype=jnp.int32)[None]
    xs = jnp.arange(NX, dtype=jnp.int32)
    moved = slots == my_slot[:, None]
    sel = jnp.where(
        moved, (source * 8 + xs * 2 + source_slot)[:, None], bal * 8 + xs[:, None] * 2 + slots
    ).reshape(8)
    own_lengths = jnp.sum(jnp.where((bals == bal)[:, :, None], lengths, 0), axis=1)
    moved_length = jnp.sum(
        jnp.where(
            is_source[:, :, None] & (slots[None] == source_slot[:, None, None]), lengths, 0
        ),
        axis=(1, 2),
    )
    proc_lengths = jnp.where(moved, moved_length[:, None], own_lengths)
    my_lengths = jnp.sum(jnp.where(xs[:, None] == x, proc_lengths, 0), axis=0)

    id_flat = id_all.reshape(64, TABLES, SLOT)
    looked = lookup(sel, id_flat, tabs.reshape(TABLES, DISTINCT, COLS))
    rows = exchange(looked.reshape(NX, 256, COLS), True)
    forward_out, grad_rows, partial_in, partial_out = layer(
        my_lengths, rows, cotangent[0], w_in.reshape(D, 4 * D), w_out.reshape(D, D)
    )
    columns = exchange(grad_rows, False)
    part = scatter(sel, id_flat, columns.reshape(1024, COLS))
    wg = jnp.concatenate([partial_in, partial_out], axis=1).reshape(NY, 2, NX, 16, 2560)
    table_sum, weight_sum = reduce_all(part.reshape(4, 4, NY, 2, 128, COLS), wg)
    events = NB * item_ids.shape[1]
    table_scale = (DISTINCT / events) ** 0.5
    grad_scale = events ** (-0.5)
    weight_sum = weight_sum.reshape(64, 2560)
    return (
        forward_out[None],
        (table_sum * table_scale)[None],
        weight_sum[:, :2048] * grad_scale,
        weight_sum[:, 2048:] * grad_scale,
    )


def solution(mesh):
    placed = (
        P("bal", None, None),
        P(None, "emb", None),
        P(None, "emb"),
        P(None, "emb"),
        P("emb", None, None),
        P("bal", None),
        P("bal", None),
        P("bal", "emb", None),
    )
    return jax.shard_map(
        on_device,
        mesh=mesh,
        in_specs=placed,
        out_specs=(P("bal", "emb", None), P("emb", "bal", None), P("bal", None), P("bal", None)),
        check_vma=False,
    )
```

```python
import functools

import jax
import jax.numpy as jnp
from jax import lax
from jax.experimental import pallas as pl
from jax.experimental.pallas import tpu as pltpu
from jax.sharding import PartitionSpec as P

D = 512
HEADS = 8
COLS = 128
DISTINCT = 1024
SLOT = 128
NSEQ = 2
TABLES = 16
NZ = 16
NX = 4
NY = 4
NB = 8
EPS = 1e-05
BF = jnp.bfloat16
F32 = jnp.float32
VMEM_LIMIT = 64000 * 1024


def place():
    emb = lax.axis_index("emb")
    bal = lax.axis_index("bal")
    return emb // NX, emb % NX, bal // 2, bal % 2


def at(z, x, y, k):
    return {"emb": z * NX + x, "bal": y * 2 + k}


def rcopy(src, dst, send, recv, device):
    return pltpu.make_async_remote_copy(
        src_ref=src,
        dst_ref=dst,
        send_sem=send,
        recv_sem=recv,
        device_id=device,
        device_id_type=pl.DeviceIdType.MESH,
    )


def greet(devices):
    barrier = pltpu.get_barrier_semaphore()
    for device in devices:
        pl.semaphore_signal(barrier, inc=1, device_id=device, device_id_type=pl.DeviceIdType.MESH)
    pl.semaphore_wait(barrier, len(devices))


VM = pl.BlockSpec(memory_space=pltpu.VMEM)
ANY = pl.BlockSpec(memory_space=pl.ANY)
DMA = pltpu.SemaphoreType.DMA


Z_SLICES = [(d, s) for s in range(1, 9) for d in (-1, 1) if d < 0 or s < 8]
Z_INDEX = {pair: i for i, pair in enumerate(Z_SLICES)}


def gather_kernel(
    tab, win, wout, ids, meta, tabs, wfi, wfo, idall, metall,
    zs, zr, ys, yr, cs, cr, ws, wr, os_, or_, is_, ir, ms, mr, loc,
):
    z, x, y, k = place()
    right, left = at((z + 1) % NZ, x, y, k), at((z + NZ - 1) % NZ, x, y, k)
    yp, ym, y2 = (y + 1) % NY, (y + 3) % NY, (y + 2) % NY
    up, down = at(z, x, yp, k), at(z, x, ym, k)
    xp, xm, x2 = (x + 1) % NX, (x + 3) % NX, (x + 2) % NX
    east, west, far = at(z, xp, y, k), at(z, xm, y, k), at(z, x2, y, k)
    other = at(z, x, y, 1 - k)
    greet([right, left, up, down, east, west, far, other])

    sent = []

    def go(src, dst, send, recv, device):
        copy = rcopy(src, dst, send, recv, device)
        copy.start()
        sent.append(copy)

    def came(dst, send, recv, device):
        rcopy(dst, dst, send, recv, device).wait_recv()

    local = [
        pltpu.make_async_copy(tab, tabs.at[z], loc.at[0]),
        pltpu.make_async_copy(win.at[x], wfi.at[y, k, x], loc.at[1]),
        pltpu.make_async_copy(wout.at[x], wfo.at[y, k, x], loc.at[2]),
        pltpu.make_async_copy(ids, idall.at[y, k], loc.at[3]),
        pltpu.make_async_copy(meta, metall.at[x], loc.at[4]),
    ]
    go(tab.at[y, k], tabs.at[z, y, k], zs.at[0], zr.at[0], right)
    go(tab.at[y, k], tabs.at[z, y, k], zs.at[1], zr.at[1], left)
    for copy in local:
        copy.start()
    for i, (peer, dev) in enumerate(((xp, east), (xm, west), (x2, far))):
        go(meta, metall.at[x], ms.at[i], mr.at[i], dev)
    go(ids, idall.at[y, k], is_.at[0], ir.at[0], up)
    go(ids, idall.at[y, k], is_.at[1], ir.at[1], down)
    go(win.at[x], wfi.at[y, k, x], ws.at[0], wr.at[0], up)
    go(win.at[x], wfi.at[y, k, x], ws.at[1], wr.at[1], down)
    go(wout.at[x], wfo.at[y, k, x], os_.at[0], or_.at[0], up)
    go(wout.at[x], wfo.at[y, k, x], os_.at[1], or_.at[1], down)

    def slot(d, s):
        return (z + d * s + NZ) % NZ

    def weights_y_relay():
        came(idall.at[ym, k], is_.at[0], ir.at[0], up)
        go(idall.at[ym, k, 0:4], idall.at[ym, k, 0:4], is_.at[2], ir.at[2], up)
        came(idall.at[yp, k], is_.at[1], ir.at[1], down)
        go(idall.at[yp, k, 4:8], idall.at[yp, k, 4:8], is_.at[3], ir.at[3], down)
        for full, s_, r_, half in ((wfi, ws, wr, 1024), (wfo, os_, or_, 256)):
            came(full.at[ym, k, x], s_.at[0], r_.at[0], up)
            part = full.at[ym, k, x, :, 0:half]
            go(part, part, s_.at[2], r_.at[2], up)
            came(full.at[yp, k, x], s_.at[1], r_.at[1], down)
            part = full.at[yp, k, x, :, half:2 * half]
            go(part, part, s_.at[3], r_.at[3], down)

    def weights_x_send():
        came(idall.at[y2, k, 0:4], is_.at[2], ir.at[2], up)
        came(idall.at[y2, k, 4:8], is_.at[3], ir.at[3], down)
        local[3].wait()
        go(idall.at[:, k], idall.at[:, k], is_.at[4], ir.at[4], other)
        local[1].wait()
        local[2].wait()
        for full, s_, r_, half in ((wfi, ws, wr, 1024), (wfo, os_, or_, 256)):
            came(full.at[y2, k, x, :, 0:half], s_.at[2], r_.at[2], up)
            came(full.at[y2, k, x, :, half:2 * half], s_.at[3], r_.at[3], down)
            go(full.at[:, k, x], full.at[:, k, x], s_.at[4], r_.at[4], east)
            go(full.at[:, k, x], full.at[:, k, x], s_.at[5], r_.at[5], west)

    def weights_x_relay():
        for full, s_, r_ in ((wfi, ws, wr), (wfo, os_, or_)):
            came(full.at[:, k, xm], s_.at[4], r_.at[4], east)
            part = full.at[0:2, k, xm]
            go(part, part, s_.at[6], r_.at[6], east)
            came(full.at[:, k, xp], s_.at[5], r_.at[5], west)
            part = full.at[2:4, k, xp]
            go(part, part, s_.at[7], r_.at[7], west)

    def weights_core():
        for full, s_, r_ in ((wfi, ws, wr), (wfo, os_, or_)):
            came(full.at[0:2, k, x2], s_.at[6], r_.at[6], east)
            came(full.at[2:4, k, x2], s_.at[7], r_.at[7], west)
            go(full.at[:, k], full.at[:, k], s_.at[8], r_.at[8], other)

    for st in range(1, 11):
        for d in (-1, 1):
            if (d, st) not in Z_INDEX:
                continue
            i, zz = Z_INDEX[(d, st)], slot(d, st)
            mine = tabs.at[zz, y, k]
            onward = right if d < 0 else left
            came(mine, zs.at[i], zr.at[i], onward)
            if (d, st + 1) in Z_INDEX:
                j = Z_INDEX[(d, st + 1)]
                go(mine, mine, zs.at[j], zr.at[j], onward)
            go(mine, mine, ys.at[i, 0], yr.at[i, 0], up)
            go(mine, mine, ys.at[i, 1], yr.at[i, 1], down)
        for d in (-1, 1):
            if (d, st - 1) not in Z_INDEX:
                continue
            i, zz = Z_INDEX[(d, st - 1)], slot(d, st - 1)
            came(tabs.at[zz, ym, k], ys.at[i, 0], yr.at[i, 0], up)
            part = tabs.at[zz, ym, k, 0:64]
            go(part, part, ys.at[i, 2], yr.at[i, 2], up)
            came(tabs.at[zz, yp, k], ys.at[i, 1], yr.at[i, 1], down)
            part = tabs.at[zz, yp, k, 64:128]
            go(part, part, ys.at[i, 3], yr.at[i, 3], down)
        for d in (-1, 1):
            if (d, st - 2) not in Z_INDEX:
                continue
            i, zz = Z_INDEX[(d, st - 2)], slot(d, st - 2)
            came(tabs.at[zz, y2, k, 0:64], ys.at[i, 2], yr.at[i, 2], up)
            came(tabs.at[zz, y2, k, 64:128], ys.at[i, 3], yr.at[i, 3], down)
            go(tabs.at[zz, :, k], tabs.at[zz, :, k], cs.at[i], cr.at[i], other)
        if st == 1:
            weights_y_relay()
        if st == 2:
            weights_x_send()
        if st == 5:
            weights_x_relay()
        if st == 8:
            weights_core()

    for i, peer in enumerate((xm, xp, x2)):
        came(metall.at[peer], ms.at[i], mr.at[i], other)
    came(idall.at[:, 1 - k], is_.at[4], ir.at[4], other)
    came(wfi.at[:, 1 - k], ws.at[8], wr.at[8], other)
    came(wfo.at[:, 1 - k], os_.at[8], or_.at[8], other)
    for (d, s), i in Z_INDEX.items():
        came(tabs.at[slot(d, s), :, 1 - k], cs.at[i], cr.at[i], other)
    for copy in sent:
        copy.wait_send()
    local[0].wait()
    local[4].wait()


def gather_all(tab, win, wout, ids, meta):
    return pl.pallas_call(
        gather_kernel,
        name="gather_all",
        out_shape=(
            jax.ShapeDtypeStruct((NZ, NY, 2, 128, COLS), BF),
            jax.ShapeDtypeStruct((NY, 2, NX, 16, 2048), BF),
            jax.ShapeDtypeStruct((NY, 2, NX, 16, 512), BF),
            jax.ShapeDtypeStruct((NY, 2, 8, TABLES, SLOT), jnp.int32),
            jax.ShapeDtypeStruct((NX, 8, 128), jnp.int32),
        ),
        in_specs=[VM] * 5,
        out_specs=(ANY,) * 5,
        scratch_shapes=[
            DMA((15,)), DMA((15,)), DMA((15, 4)), DMA((15, 4)), DMA((15,)), DMA((15,)),
            DMA((9,)), DMA((9,)), DMA((9,)), DMA((9,)), DMA((5,)), DMA((5,)),
            DMA((3,)), DMA((3,)), DMA((5,)),
        ],
        compiler_params=pltpu.CompilerParams(collective_id=0, has_side_effects=True),
    )(tab, win, wout, ids, meta)


def lookup_kernel(sel, *refs):
    slots, (table, out, rows, columns, total) = refs[:8], refs[8:]
    t = pl.program_id(0)

    @pl.when(t == 0)
    def _():
        for i in range(8):
            rows[:, i * SLOT:(i + 1) * SLOT] = slots[i][0]
            columns[i * SLOT:(i + 1) * SLOT, :] = jnp.transpose(slots[i][0])
        total[...] = jnp.zeros_like(total)

    lane = lax.broadcasted_iota(jnp.int32, (8 * SLOT, TABLES), 1)
    picked = jnp.sum(jnp.where(lane == t, columns[...], 0), axis=1, keepdims=True)
    acc = total[...]
    for part in range(4):
        vocab = lax.broadcasted_iota(jnp.int32, (8 * SLOT, 256), 1) + part * 256
        hot = jnp.where(picked == vocab, 1.0, 0.0).astype(BF)
        acc = acc + jnp.dot(
            hot, table[0, part * 256:(part + 1) * 256, :], preferred_element_type=F32
        )
    total[...] = acc

    @pl.when(t == TABLES - 1)
    def _():
        out[...] = acc.astype(BF)


def slot_spec(i):
    return pl.BlockSpec((1, TABLES, SLOT), lambda t, sel: (sel[i], 0, 0))


def lookup(sel, ids, tables):
    return pl.pallas_call(
        lookup_kernel,
        name="lookup",
        out_shape=(
            jax.ShapeDtypeStruct((8 * SLOT, COLS), BF),
            jax.ShapeDtypeStruct((TABLES, 8 * SLOT), jnp.int32),
        ),
        grid_spec=pltpu.PrefetchScalarGridSpec(
            num_scalar_prefetch=1,
            grid=(TABLES,),
            in_specs=[slot_spec(i) for i in range(8)]
            + [pl.BlockSpec((1, DISTINCT, COLS), lambda t, sel: (t, 0, 0))],
            out_specs=(
                pl.BlockSpec((8 * SLOT, COLS), lambda t, sel: (0, 0)),
                pl.BlockSpec((TABLES, 8 * SLOT), lambda t, sel: (0, 0)),
            ),
            scratch_shapes=[
                pltpu.VMEM((8 * SLOT, TABLES), jnp.int32),
                pltpu.VMEM((8 * SLOT, COLS), F32),
            ],
        ),
    )(sel, *([ids] * 8), tables)


def exchange_kernel(src, out, send, recv, loc):
    z, x, y, k = place()
    peers = [(x + 1) % NX, (x + 3) % NX, (x + 2) % NX]
    devices = [at(z, peer, y, k) for peer in peers]
    greet(devices)

    def piece(i):
        return out.at[:, pl.ds(pl.multiple_of(i * COLS, COLS), COLS)]

    copies = []
    for i, (peer, device) in enumerate(zip(peers, devices)):
        copy = rcopy(src.at[peer], piece(x), send.at[i], recv.at[i], device)
        copy.start()
        copies.append(copy)
    own = pltpu.make_async_copy(src.at[x], piece(x), loc)
    own.start()
    for i, source in enumerate((peers[1], peers[0], peers[2])):
        landed = piece(source)
        rcopy(landed, landed, send.at[i], recv.at[i], devices[i]).wait_recv()
    for copy in copies:
        copy.wait_send()
    own.wait()


def exchange(array):
    return pl.pallas_call(
        exchange_kernel,
        name="exchange_rows",
        out_shape=jax.ShapeDtypeStruct((256, D), BF),
        in_specs=[VM],
        out_specs=VM,
        scratch_shapes=[DMA((3,)), DMA((3,)), DMA],
        compiler_params=pltpu.CompilerParams(collective_id=1, has_side_effects=True),
    )(array)


OFFSETS = (2, 1, -1, 0)
FAR_FIRST = (8, 7, 9, 6, 10, 5, 11, 4, 12, 3, 13, 2, 14, 1, 15)


def back_kernel(
    table_scale, grad_scale,
    grads, rows, wg, tout, win_out, wout_out,
    gx, to, t1, ta, tl1, tr1, tl2, tr2, tb, tz1, ts, tz2,
    w1, wa, wl1, wr1, wl2, wr2, wb, vl1, vr1, vl2, vr2, wc, wz, wd, we,
    gs, gr, cs, cr, ys, yr, zs, zr, z2s, z2r, loc,
    wcs, wcr, wxs, wxr, wys, wyr, wzs, wzr, wgs, wgr, wes, wer,
):
    z, x, y, k = place()
    yp, ym, y2 = (y + 1) % NY, (y + 3) % NY, (y + 2) % NY
    xp, xm, x2 = (x + 1) % NX, (x + 3) % NX, (x + 2) % NX
    up, down = at(z, x, yp, k), at(z, x, ym, k)
    east, west, far = at(z, xp, y, k), at(z, xm, y, k), at(z, x2, y, k)
    other = at(z, x, y, 1 - k)
    ring = {o: (z + o) % NZ for o in range(1, NZ)}
    greet([up, down, east, west, far, other] + [at(ring[o], x, y, k) for o in range(1, NZ)])

    sent = []

    def go(src, dst, send, recv, device):
        copy = rcopy(src, dst, send, recv, device)
        copy.start()
        sent.append(copy)

    def came(dst, send, recv):
        rcopy(dst, dst, send, recv, other).wait_recv()

    def add(*values):
        total = values[0].astype(F32)
        for value in values[1:]:
            total = total + value.astype(F32)
        return total

    def columns(i):
        return grads.at[:, pl.ds(pl.multiple_of(i * COLS, COLS), COLS)]

    for i, (peer, device) in enumerate(((x2, far), (xp, east), (xm, west))):
        go(columns(peer), gx.at[x], gs.at[i], gr.at[i], device)
    own = pltpu.make_async_copy(columns(x), gx.at[x], loc.at[0])
    own.start()
    go(wg.at[:, 1 - k], w1, wcs, wcr, other)
    wload = pltpu.make_async_copy(wg.at[:, k], wa, loc.at[1])
    wload.start()

    place_row = lax.broadcasted_iota(jnp.int32, (128, 8 * SLOT), 0)

    def rows_of(q, core, out):
        residue = (z + OFFSETS[q] + NZ) % 4

        def body(i, carry):
            picked = rows[pl.ds(i * 4 + residue, 1), :] - core * 128
            hot = jnp.concatenate(
                [
                    jnp.where(picked - part * 256 == place_row, 1.0, 0.0).astype(BF)
                    for part in range(4)
                ],
                axis=0,
            )
            found = jnp.dot(
                hot, gx[...].reshape(8 * SLOT, COLS), preferred_element_type=F32
            ).astype(BF)
            out[q, i] = found.reshape(NY, 128, COLS)
            return carry

        lax.fori_loop(0, 4, body, 0)

    def compute(q):
        rows_of(q, 1 - k, to)
        go(to.at[q], t1.at[q], cs.at[q], cr.at[q], other)
        rows_of(q, k, ta)

    def t_core(q):
        came(t1.at[q], cs.at[q], cr.at[q])
        for i in range(4):
            ta[q, i] = add(ta[q, i], t1[q, i]).astype(BF)
        go(ta.at[q, :, y2, 0:64], tl1.at[q], ys.at[q, 0], yr.at[q, 0], up)
        go(ta.at[q, :, y2, 64:128], tr1.at[q], ys.at[q, 1], yr.at[q, 1], down)

    def t_y(q):
        came(tl1.at[q], ys.at[q, 0], yr.at[q, 0])
        ta[q, :, yp, 0:64] = add(ta[q, :, yp, 0:64], tl1[q]).astype(BF)
        go(ta.at[q, :, yp], tl2.at[q], ys.at[q, 2], yr.at[q, 2], up)
        came(tr1.at[q], ys.at[q, 1], yr.at[q, 1])
        ta[q, :, ym, 64:128] = add(ta[q, :, ym, 64:128], tr1[q]).astype(BF)
        go(ta.at[q, :, ym], tr2.at[q], ys.at[q, 3], yr.at[q, 3], down)

    def t_z(q):
        came(tl2.at[q], ys.at[q, 2], yr.at[q, 2])
        came(tr2.at[q], ys.at[q, 3], yr.at[q, 3])
        tb[q] = add(ta[q, :, y], tl2[q], tr2[q]).astype(BF)
        if q < 3:
            device = at((z + OFFSETS[q] + NZ) % NZ, x, y, k)
            go(tb.at[q], tz1.at[q], zs.at[q], zr.at[q], device)

    def t_z2():
        for q in range(3):
            came(tz1.at[q], zs.at[q], zr.at[q])
        ts[...] = add(tb[3], tz1[0], tz1[1], tz1[2]).astype(BF)
        for m in (2, 1, 3):
            zz = (z + 4 * m) % NZ
            go(ts.at[zz // 4], tz2.at[m - 1], z2s.at[m - 1], z2r.at[m - 1], at(zz, x, y, k))

    def t_end():
        total = ts[z // 4].astype(F32)
        for m in range(3):
            came(tz2.at[m], z2s.at[m], z2r.at[m])
            total = total + tz2[m].astype(F32)
        tout[...] = total * table_scale

    def w_core():
        wload.wait()
        came(w1, wcs, wcr)
        for i in range(4):
            wa[i] = add(wa[i], w1[i]).astype(BF)
        go(wa.at[0:2, x2], wl1, wxs.at[0], wxr.at[0], east)
        go(wa.at[2:4, x2], wr1, wxs.at[1], wxr.at[1], west)

    def w_x():
        came(wl1, wxs.at[0], wxr.at[0])
        wa[0:2, xp] = add(wa[0:2, xp], wl1[...]).astype(BF)
        go(wa.at[:, xp], wl2, wxs.at[2], wxr.at[2], east)
        came(wr1, wxs.at[1], wxr.at[1])
        wa[2:4, xm] = add(wa[2:4, xm], wr1[...]).astype(BF)
        go(wa.at[:, xm], wr2, wxs.at[3], wxr.at[3], west)

    def w_x2():
        came(wl2, wxs.at[2], wxr.at[2])
        came(wr2, wxs.at[3], wxr.at[3])
        wb[...] = add(wa[:, x], wl2[...], wr2[...]).astype(BF)
        go(wb.at[y2, :, 0:1280], vl1, wys.at[0], wyr.at[0], up)
        go(wb.at[y2, :, 1280:2560], vr1, wys.at[1], wyr.at[1], down)

    def w_y():
        came(vl1, wys.at[0], wyr.at[0])
        wb[yp, :, 0:1280] = add(wb[yp, :, 0:1280], vl1[...]).astype(BF)
        go(wb.at[yp], vl2, wys.at[2], wyr.at[2], up)
        came(vr1, wys.at[1], wyr.at[1])
        wb[ym, :, 1280:2560] = add(wb[ym, :, 1280:2560], vr1[...]).astype(BF)
        go(wb.at[ym], vr2, wys.at[3], wyr.at[3], down)

    def w_y2():
        came(vl2, wys.at[2], wyr.at[2])
        came(vr2, wys.at[3], wyr.at[3])
        summed = add(wb[y], vl2[...], vr2[...]).astype(BF)
        for j in range(NZ):
            wc[j, 0] = summed[:, j * 128:(j + 1) * 128]
            c = 16 + j // 4
            wc[j, 1] = summed[:, c * 128:(c + 1) * 128]
        for o in FAR_FIRST:
            zz = ring[o]
            go(wc.at[zz], wz.at[o - 1], wzs.at[o - 1], wzr.at[o - 1], at(zz, x, y, k))

    def w_z():
        total = wc[z].astype(F32)
        for o in range(1, NZ):
            came(wz.at[o - 1], wzs.at[o - 1], wzr.at[o - 1])
            total = total + wz[o - 1].astype(F32)
        wd[z] = total.astype(BF)
        for o in FAR_FIRST:
            go(wd.at[z], wd.at[z], wgs.at[o - 1], wgr.at[o - 1], at(ring[o], x, y, k))

    def w_z2():
        for o in range(1, NZ):
            came(wd.at[(z + NZ - o) % NZ], wgs.at[o - 1], wgr.at[o - 1])
        for j in range(16):
            we[x, :, j * 128:(j + 1) * 128] = wd[j, 0]
        for c in range(4):
            we[x, :, 2048 + c * 128:2048 + (c + 1) * 128] = wd[4 * c, 1]
        go(we.at[x], we.at[x], wes.at[0], wer.at[0], east)
        go(we.at[x], we.at[x], wes.at[1], wer.at[1], west)

    def w_x3():
        came(we.at[xm], wes.at[0], wer.at[0])
        part = we.at[xm, :, 0:1280]
        go(part, part, wes.at[2], wer.at[2], east)
        came(we.at[xp], wes.at[1], wer.at[1])
        part = we.at[xp, :, 1280:2560]
        go(part, part, wes.at[3], wer.at[3], west)

    def w_end():
        came(we.at[x2, :, 0:1280], wes.at[2], wer.at[2])
        came(we.at[x2, :, 1280:2560], wes.at[3], wer.at[3])
        for i in range(NX):
            total = we[i].astype(F32) * grad_scale
            win_out[i * 16:(i + 1) * 16, :] = total[:, :2048]
            wout_out[i * 16:(i + 1) * 16, :] = total[:, 2048:]

    own.wait()
    for i, source in enumerate((x2, xm, xp)):
        came(gx.at[source], gs.at[i], gr.at[i])
    compute(0)
    w_core()
    t_core(0)
    compute(1)
    w_x()
    t_y(0)
    t_core(1)
    compute(2)
    w_x2()
    t_z(0)
    t_y(1)
    t_core(2)
    compute(3)
    w_y()
    t_z(1)
    t_y(2)
    t_core(3)
    w_y2()
    t_z(2)
    t_y(3)
    w_z()
    t_z(3)
    t_z2()
    w_z2()
    w_x3()
    t_end()
    w_end()
    for copy in sent:
        copy.wait_send()


def back(grads, rows, wg, table_scale, grad_scale):
    v = pltpu.VMEM
    return pl.pallas_call(
        functools.partial(back_kernel, table_scale, grad_scale),
        name="back",
        out_shape=(
            jax.ShapeDtypeStruct((128, COLS), F32),
            jax.ShapeDtypeStruct((64, 2048), F32),
            jax.ShapeDtypeStruct((64, 512), F32),
        ),
        in_specs=[VM] * 3,
        out_specs=(VM,) * 3,
        scratch_shapes=[
            v((NX, 256, COLS), BF), v((4, 4, NY, 128, COLS), BF),
            v((4, 4, NY, 128, COLS), BF), v((4, 4, NY, 128, COLS), BF),
            v((4, 4, 64, COLS), BF), v((4, 4, 64, COLS), BF),
            v((4, 4, 128, COLS), BF), v((4, 4, 128, COLS), BF),
            v((4, 4, 128, COLS), BF), v((3, 4, 128, COLS), BF),
            v((4, 128, COLS), BF), v((3, 128, COLS), BF),
            v((NY, NX, 16, 2560), BF), v((NY, NX, 16, 2560), BF),
            v((2, 16, 2560), BF), v((2, 16, 2560), BF),
            v((4, 16, 2560), BF), v((4, 16, 2560), BF), v((4, 16, 2560), BF),
            v((16, 1280), BF), v((16, 1280), BF), v((16, 2560), BF), v((16, 2560), BF),
            v((NZ, 2, 16, 128), BF), v((15, 2, 16, 128), BF),
            v((NZ, 2, 16, 128), BF), v((NX, 16, 2560), BF),
            DMA((3,)), DMA((3,)),
            DMA((4,)), DMA((4,)), DMA((4, 4)), DMA((4, 4)), DMA((3,)), DMA((3,)),
            DMA((3,)), DMA((3,)), DMA((2,)),
            DMA, DMA, DMA((4,)), DMA((4,)), DMA((4,)), DMA((4,)),
            DMA((15,)), DMA((15,)), DMA((15,)), DMA((15,)), DMA((4,)), DMA((4,)),
        ],
        compiler_params=pltpu.CompilerParams(
            collective_id=3, has_side_effects=True, vmem_limit_bytes=VMEM_LIMIT
        ),
    )(grads, rows, wg)


def silu_grad(argument):
    logistic = jax.nn.sigmoid(argument)
    return logistic * (1.0 + argument * (1.0 - logistic))


def normalize(values):
    average = jnp.mean(values, axis=1, keepdims=True)
    centred = values - average
    inverse = lax.rsqrt(jnp.mean(centred * centred, axis=1, keepdims=True) + EPS)
    return centred * inverse, inverse


def norm_back(incoming, normed, inverse):
    first = jnp.mean(incoming, axis=1, keepdims=True)
    second = jnp.mean(incoming * normed, axis=1, keepdims=True)
    return inverse * (incoming - first - normed * second)


def dot(a, b, ca, cb):
    return lax.dot_general(a, b, (((ca,), (cb,)), ((), ())), preferred_element_type=F32)


def layer_kernel(lengths, rows, cot, w_in, w_out, out, grad, wg, act, proj, att, gh):
    width = D // HEADS
    scale = width ** (-0.5)
    values = rows[...].astype(F32)
    normed_in, in_inverse = normalize(values)
    half_in = normed_in.astype(BF)
    projected = dot(half_in, w_in[...], 1, 0)
    proj[...] = projected
    activated = jax.nn.silu(projected)
    gate = activated[:, :D]
    act[...] = activated[:, D:].astype(BF)
    place_i = lax.broadcasted_iota(jnp.int32, (SLOT, SLOT), 0)
    place_j = lax.broadcasted_iota(jnp.int32, (SLOT, SLOT), 1)
    masks = [(place_j <= place_i) & (place_i < lengths[s]) for s in range(NSEQ)]

    def heads(s, h):
        r = slice(s * SLOT, (s + 1) * SLOT)
        v = act[r, h * width:(h + 1) * width]
        q = act[r, D + h * width:D + (h + 1) * width]
        key = act[r, 2 * D + h * width:2 * D + (h + 1) * width]
        return r, v, q, key

    for s in range(NSEQ):
        for h in range(HEADS):
            r, v, q, key = heads(s, h)
            scores = dot(q, key, 1, 1) * scale
            weights = jnp.where(masks[s], jax.nn.silu(scores) * (1.0 / SLOT), 0.0).astype(BF)
            att[r, h * width:(h + 1) * width] = dot(weights, v, 1, 0)
    normed_out, out_inverse = normalize(att[...])
    mixed = (normed_out * gate).astype(BF)
    out[...] = (values + dot(mixed, w_out[...], 1, 0)).astype(BF)
    cotangent = cot[...]
    wg[:, 4 * D:] = dot(mixed, cotangent, 0, 0).astype(BF)
    grad_mixed = dot(cotangent, w_out[...], 1, 1)
    att[...] = norm_back(grad_mixed * gate, normed_out, out_inverse)
    gh[:, :D] = (grad_mixed * normed_out * silu_grad(proj[:, :D])).astype(BF)
    for s in range(NSEQ):
        for h in range(HEADS):
            r, v, q, key = heads(s, h)
            g = att[r, h * width:(h + 1) * width].astype(BF)
            scores = dot(q, key, 1, 1) * scale
            logistic = jax.nn.sigmoid(scores)
            weights = jnp.where(masks[s], scores * logistic * (1.0 / SLOT), 0.0).astype(BF)
            slope = logistic * (1.0 + scores * (1.0 - logistic))
            gw = dot(g, v, 1, 1)
            gs = jnp.where(masks[s], gw * (1.0 / SLOT) * slope, 0.0).astype(BF)
            parts = (
                dot(weights, g, 0, 0), dot(gs, key, 1, 0) * scale, dot(gs, q, 0, 0) * scale
            )
            for p in range(3):
                c = slice(D + p * D + h * width, D + p * D + (h + 1) * width)
                gh[r, c] = (parts[p] * silu_grad(proj[r, c])).astype(BF)
    grad_projected = gh[...]
    wg[:, :4 * D] = dot(half_in, grad_projected, 0, 0).astype(BF)
    grad_normed = dot(grad_projected, w_in[...], 1, 1)
    grad[...] = (
        cotangent.astype(F32) + norm_back(grad_normed, normed_in, in_inverse)
    ).astype(BF)


def layer(lengths, rows, cot, w_in, w_out):
    v = pltpu.VMEM
    return pl.pallas_call(
        layer_kernel,
        name="layer",
        out_shape=(
            jax.ShapeDtypeStruct((256, D), BF),
            jax.ShapeDtypeStruct((256, D), BF),
            jax.ShapeDtypeStruct((D, 5 * D), BF),
        ),
        in_specs=[pl.BlockSpec(memory_space=pltpu.SMEM)] + [VM] * 4,
        out_specs=(VM,) * 3,
        scratch_shapes=[
            v((256, 3 * D), BF), v((256, 4 * D), F32), v((256, D), F32), v((256, 4 * D), BF),
        ],
        compiler_params=pltpu.CompilerParams(vmem_limit_bytes=VMEM_LIMIT),
    )(lengths, rows, cot, w_in, w_out)


def on_device(
    item_ids, seq_lengths, surplus_slot, helper_map, embed_tables, weight_in, weight_out, cotangent
):
    z, x, y, k = place()
    bal = lax.axis_index("bal")
    near = lax.dynamic_slice_in_dim(item_ids[0], z * 1024, 1024, 0)
    ids = jnp.transpose(near.reshape(8, SLOT, TABLES), (0, 2, 1))
    meta = jnp.concatenate(
        [seq_lengths.reshape(16), surplus_slot.reshape(8), helper_map.reshape(8)]
    )
    meta = jnp.broadcast_to(jnp.pad(meta, (0, 96))[None], (8, 128))
    tabs, w_in, w_out, id_all, meta_all = gather_all(
        embed_tables.reshape(NY, 2, 128, COLS),
        weight_in.reshape(NX, 16, 2048),
        weight_out.reshape(NX, 16, 512),
        ids,
        meta,
    )
    facts = meta_all[:, 0, :32]
    lengths = facts[:, :16].reshape(NX, NB, NSEQ)
    surplus = facts[:, 16:24]
    helper = facts[:, 24:32]
    bals = jnp.arange(NB, dtype=jnp.int32)[None]
    is_source = helper == bal
    source = jnp.sum(jnp.where(is_source, bals, 0), axis=1)
    source_slot = jnp.sum(jnp.where(is_source, surplus, 0), axis=1)
    my_slot = jnp.sum(jnp.where(bals == bal, surplus, 0), axis=1)
    slots = jnp.arange(NSEQ, dtype=jnp.int32)[None]
    xs = jnp.arange(NX, dtype=jnp.int32)
    moved = slots == my_slot[:, None]
    sel = jnp.where(
        moved, (source * 8 + xs * 2 + source_slot)[:, None], bal * 8 + xs[:, None] * 2 + slots
    ).reshape(8)
    own_lengths = jnp.sum(jnp.where((bals == bal)[:, :, None], lengths, 0), axis=1)
    moved_length = jnp.sum(
        jnp.where(
            is_source[:, :, None] & (slots[None] == source_slot[:, None, None]), lengths, 0
        ),
        axis=(1, 2),
    )
    proc_lengths = jnp.where(moved, moved_length[:, None], own_lengths)
    my_lengths = jnp.sum(jnp.where(xs[:, None] == x, proc_lengths, 0), axis=0)

    id_flat = id_all.reshape(64, TABLES, SLOT)
    looked, id_rows = lookup(sel, id_flat, tabs.reshape(TABLES, DISTINCT, COLS))
    rows = exchange(looked.reshape(NX, 256, COLS))
    forward_out, grad_rows, wg = layer(
        my_lengths, rows, cotangent[0], w_in.reshape(D, 4 * D), w_out.reshape(D, D)
    )
    events = NB * item_ids.shape[1]
    table_grad, grad_in, grad_out = back(
        grad_rows,
        id_rows,
        wg.reshape(NY, 2, NX, 16, 2560),
        (DISTINCT / events) ** 0.5,
        events ** (-0.5),
    )
    return forward_out[None], table_grad[None], grad_in, grad_out


def solution(mesh):
    placed = (
        P("bal", None, None),
        P(None, "emb", None),
        P(None, "emb"),
        P(None, "emb"),
        P("emb", None, None),
        P("bal", None),
        P("bal", None),
        P("bal", "emb", None),
    )
    return jax.shard_map(
        on_device,
        mesh=mesh,
        in_specs=placed,
        out_specs=(P("bal", "emb", None), P("emb", "bal", None), P("bal", None), P("bal", None)),
        check_vma=False,
    )
```

```python
import functools

import jax
import jax.numpy as jnp
from jax import lax
from jax.experimental import pallas as pl
from jax.experimental.pallas import tpu as pltpu
from jax.sharding import PartitionSpec as P

D = 512
HEADS = 8
COLS = 128
DISTINCT = 1024
SLOT = 128
NSEQ = 2
TABLES = 16
NZ = 16
NX = 4
NY = 4
NB = 8
EPS = 1e-05
BF = jnp.bfloat16
F32 = jnp.float32
VMEM_LIMIT = 64000 * 1024


def place():
    emb = lax.axis_index("emb")
    bal = lax.axis_index("bal")
    return emb // NX, emb % NX, bal // 2, bal % 2


def at(z, x, y, k):
    return {"emb": z * NX + x, "bal": y * 2 + k}


def rcopy(src, dst, send, recv, device):
    return pltpu.make_async_remote_copy(
        src_ref=src,
        dst_ref=dst,
        send_sem=send,
        recv_sem=recv,
        device_id=device,
        device_id_type=pl.DeviceIdType.MESH,
    )


def greet(devices):
    barrier = pltpu.get_barrier_semaphore()
    for device in devices:
        pl.semaphore_signal(barrier, inc=1, device_id=device, device_id_type=pl.DeviceIdType.MESH)
    pl.semaphore_wait(barrier, len(devices))


VM = pl.BlockSpec(memory_space=pltpu.VMEM)
ANY = pl.BlockSpec(memory_space=pl.ANY)
DMA = pltpu.SemaphoreType.DMA


NEAR = (1, 15, 2)
JUMPS = (4, 12, 8)
ARRIVALS = [(0, r) for r in NEAR] + [(j, 0) for j in JUMPS] + [(j, r) for j in JUMPS for r in NEAR]
INDEX = {pair: i for i, pair in enumerate(ARRIVALS)}


def front_kernel(
    tab, win, wout, ids, meta, out, id_rows, lens, wfi, wfo,
    tabs, idall, metall, columns, total, looked,
    zs, zr, ys, yr, cs, cr, ws, wr, os_, or_, is_, ir, ms, mr, es, er, loc,
):
    z, x, y, k = place()
    bal = y * 2 + k
    y_peers = [(y + 1) % NY, (y + 3) % NY, (y + 2) % NY]
    x_peers = [(x + 1) % NX, (x + 3) % NX, (x + 2) % NX]
    y_from = [y_peers[1], y_peers[0], y_peers[2]]
    x_from = [x_peers[1], x_peers[0], x_peers[2]]
    y_devices = [at(z, x, peer, k) for peer in y_peers]
    x_devices = [at(z, peer, y, k) for peer in x_peers]
    other = at(z, x, y, 1 - k)
    offsets = NEAR + JUMPS
    z_devices = {o: at((z + o) % NZ, x, y, k) for o in offsets}
    z_sources = [at((z + NZ - o) % NZ, x, y, k) for o in (2, )]
    greet(list(z_devices.values()) + z_sources + y_devices + x_devices + [other])

    sent = []

    def go(src, dst, send, recv, device):
        copy = rcopy(src, dst, send, recv, device)
        copy.start()
        sent.append(copy)

    def came(dst, send, recv):
        rcopy(dst, dst, send, recv, other).wait_recv()

    def origin(pair):
        return (z + 2 * NZ - pair[0] - pair[1]) % NZ

    for o in JUMPS:
        i = INDEX[(o, 0)]
        go(tab.at[y, k], tabs.at[z, y, k], zs.at[i], zr.at[i], z_devices[o])
    for o in NEAR:
        i = INDEX[(0, o)]
        go(tab.at[y, k], tabs.at[z, y, k], zs.at[i], zr.at[i], z_devices[o])
    for i in range(3):
        go(ids, idall.at[y, k], is_.at[i], ir.at[i], y_devices[i])
        go(meta, metall.at[x], ms.at[i], mr.at[i], x_devices[i])
    for i in range(3):
        go(win.at[x], wfi.at[y, k, x], ws.at[i], wr.at[i], y_devices[i])
        go(wout.at[x], wfo.at[y, k, x], os_.at[i], or_.at[i], y_devices[i])
    local = [
        pltpu.make_async_copy(win.at[x], wfi.at[y, k, x], loc.at[0]),
        pltpu.make_async_copy(wout.at[x], wfo.at[y, k, x], loc.at[1]),
        pltpu.make_async_copy(ids, idall.at[y, k], loc.at[2]),
        pltpu.make_async_copy(meta, metall.at[x], loc.at[3]),
    ]
    for copy in local:
        copy.start()

    def from_z(pair):
        i, zz = INDEX[pair], origin(pair)
        mine = tabs.at[zz, y, k]
        came(mine, zs.at[i], zr.at[i])
        if pair[1] == 0:
            for r in NEAR:
                j = INDEX[(pair[0], r)]
                go(mine, mine, zs.at[j], zr.at[j], z_devices[r])
        for p in range(3):
            go(mine, mine, ys.at[i, p], yr.at[i, p], y_devices[p])

    def from_y(pair):
        i, zz = INDEX[pair], origin(pair)
        for p in range(3):
            came(tabs.at[zz, y_from[p], k], ys.at[i, p], yr.at[i, p])
        go(tabs.at[zz, :, k], tabs.at[zz, :, k], cs.at[i], cr.at[i], other)

    def from_core(pair):
        i, zz = INDEX[pair], origin(pair)
        came(tabs.at[zz, :, 1 - k], cs.at[i], cr.at[i])

    lane = lax.broadcasted_iota(jnp.int32, (8 * SLOT, TABLES), 1)
    vocab = lax.broadcasted_iota(jnp.int32, (8 * SLOT, 256), 1)

    def sum_table(t, read):
        picked = jnp.sum(jnp.where(lane == t, columns[...], 0), axis=1, keepdims=True)

        def body(part, carry):
            hot = jnp.where(picked - part * 256 == vocab, 1.0, 0.0).astype(BF)
            total[...] += jnp.dot(hot, read(part), preferred_element_type=F32)
            return carry

        lax.fori_loop(0, 4, body, 0)

    def read_own(part):
        return tab[part].reshape(256, COLS)

    def choose_ids():
        for i in range(3):
            came(metall.at[x_from[i]], ms.at[i], mr.at[i])
        local[3].wait()
        came(idall.at[:, 1 - k], is_.at[3], ir.at[3])
        for xx in range(NX):
            mine = jnp.zeros((1, SLOT), jnp.int32)
            moved = jnp.zeros((TABLES, SLOT), jnp.int32)
            for b in range(NB):
                surplus = metall[xx, 16 + b:17 + b, :]
                is_mine = jnp.where(bal == b, 1, 0)
                mine = mine + surplus * is_mine
                sends = jnp.where(metall[xx, 24 + b:25 + b, :] == bal, 1, 0)
                first = idall[b // 2, b % 2, 2 * xx]
                second = idall[b // 2, b % 2, 2 * xx + 1]
                moved = moved + sends * (first + surplus * (second - first))
            for s in range(NSEQ):
                away = mine if s == 1 else 1 - mine
                kept = idall[y, k, 2 * xx + s]
                chosen = kept + away * (moved - kept)
                i = 2 * xx + s
                id_rows[:, i * SLOT:(i + 1) * SLOT] = chosen
                columns[i * SLOT:(i + 1) * SLOT, :] = jnp.transpose(chosen)
        mine = jnp.zeros((1, SLOT), jnp.int32)
        moved = jnp.zeros((1, SLOT), jnp.int32)
        kept = [jnp.zeros((1, SLOT), jnp.int32) for _ in range(NSEQ)]
        for b in range(NB):
            surplus = metall[x, 16 + b:17 + b, :]
            is_mine = jnp.where(bal == b, 1, 0)
            mine = mine + surplus * is_mine
            sends = jnp.where(metall[x, 24 + b:25 + b, :] == bal, 1, 0)
            first = metall[x, 2 * b:2 * b + 1, :]
            second = metall[x, 2 * b + 1:2 * b + 2, :]
            moved = moved + sends * (first + surplus * (second - first))
            kept[0] = kept[0] + is_mine * first
            kept[1] = kept[1] + is_mine * second
        lens[...] = jnp.zeros_like(lens)
        lens[0:1, :] = kept[0] + (1 - mine) * (moved - kept[0])
        lens[1:2, :] = kept[1] + mine * (moved - kept[1])

    def ids_core():
        local[2].wait()
        for i in range(3):
            came(idall.at[y_from[i], k], is_.at[i], ir.at[i])
        go(idall.at[:, k], idall.at[:, k], is_.at[3], ir.at[3], other)

    def weights_x():
        local[0].wait()
        local[1].wait()
        for full, s_, r_ in ((wfi, ws, wr), (wfo, os_, or_)):
            for i in range(3):
                came(full.at[y_from[i], k, x], s_.at[i], r_.at[i])
            for i in range(3):
                part = full.at[:, k, x]
                go(part, part, s_.at[3 + i], r_.at[3 + i], x_devices[i])

    def weights_core():
        for full, s_, r_ in ((wfi, ws, wr), (wfo, os_, or_)):
            for i in range(3):
                came(full.at[:, k, x_from[i]], s_.at[3 + i], r_.at[3 + i])
            go(full.at[:, k], full.at[:, k], s_.at[6], r_.at[6], other)

    total[...] = jnp.zeros_like(total)
    for pair in ARRIVALS[:3]:
        from_z(pair)
    ids_core()
    for pair in ARRIVALS[3:6]:
        from_z(pair)
    choose_ids()
    sum_table(z, read_own)
    weights_x()
    for pair in ARRIVALS[6:9]:
        from_z(pair)
    from_y(ARRIVALS[0])
    for n in range(15):
        if n < 3:
            for pair in ARRIVALS[9 + 2 * n:11 + 2 * n]:
                from_z(pair)
        if n < 14:
            from_y(ARRIVALS[n + 1])
        if n == 13:
            weights_core()
        from_core(ARRIVALS[n])
        zz = origin(ARRIVALS[n])
        sum_table(zz, lambda part, zz=zz: tabs[zz, part].reshape(256, COLS))

    looked[...] = total[...].astype(BF).reshape(NX, 256, COLS)

    def piece(i):
        return out.at[:, pl.ds(pl.multiple_of(i * COLS, COLS), COLS)]

    for i in (2, 0, 1):
        go(looked.at[x_peers[i]], piece(x), es.at[i], er.at[i], x_devices[i])
    own = pltpu.make_async_copy(looked.at[x], piece(x), loc.at[4])
    own.start()
    came(wfi.at[:, 1 - k], ws.at[6], wr.at[6])
    came(wfo.at[:, 1 - k], os_.at[6], or_.at[6])
    for i in range(3):
        came(piece(x_from[i]), es.at[i], er.at[i])
    own.wait()
    for copy in sent:
        copy.wait_send()


def front(tab, win, wout, ids, meta):
    v = pltpu.VMEM
    return pl.pallas_call(
        front_kernel,
        name="front",
        out_shape=(
            jax.ShapeDtypeStruct((256, D), BF),
            jax.ShapeDtypeStruct((TABLES, 8 * SLOT), jnp.int32),
            jax.ShapeDtypeStruct((8, SLOT), jnp.int32),
            jax.ShapeDtypeStruct((NY, 2, NX, 16, 2048), BF),
            jax.ShapeDtypeStruct((NY, 2, NX, 16, 512), BF),
        ),
        in_specs=[VM] * 5,
        out_specs=(VM, VM, VM, ANY, ANY),
        scratch_shapes=[
            v((NZ, NY, 2, 128, COLS), BF),
            v((NY, 2, 8, TABLES, SLOT), jnp.int32),
            v((NX, 32, 128), jnp.int32),
            v((8 * SLOT, TABLES), jnp.int32),
            v((8 * SLOT, COLS), F32),
            v((NX, 256, COLS), BF),
            DMA((15,)), DMA((15,)), DMA((15, 3)), DMA((15, 3)), DMA((15,)), DMA((15,)),
            DMA((7,)), DMA((7,)), DMA((7,)), DMA((7,)), DMA((4,)), DMA((4,)),
            DMA((3,)), DMA((3,)), DMA((3,)), DMA((3,)), DMA((5,)),
        ],
        compiler_params=pltpu.CompilerParams(
            collective_id=0, has_side_effects=True, vmem_limit_bytes=VMEM_LIMIT
        ),
    )(tab, win, wout, ids, meta)


OFFSETS = (2, 1, -1, 0)
FAR_FIRST = (8, 7, 9, 6, 10, 5, 11, 4, 12, 3, 13, 2, 14, 1, 15)


def back_kernel(
    table_scale, grad_scale,
    grads, rows, wg, tout, win_out, wout_out,
    gx, to, t1, ta, tl1, tr1, tl2, tr2, tb, tz1, ts, tz2,
    w1, wa, wl1, wr1, wl2, wr2, wb, vl1, vr1, vl2, vr2, wc, wz, wd, we,
    gs, gr, cs, cr, ys, yr, zs, zr, z2s, z2r, loc,
    wcs, wcr, wxs, wxr, wys, wyr, wzs, wzr, wgs, wgr, wes, wer,
):
    z, x, y, k = place()
    yp, ym, y2 = (y + 1) % NY, (y + 3) % NY, (y + 2) % NY
    xp, xm, x2 = (x + 1) % NX, (x + 3) % NX, (x + 2) % NX
    up, down = at(z, x, yp, k), at(z, x, ym, k)
    east, west, far = at(z, xp, y, k), at(z, xm, y, k), at(z, x2, y, k)
    other = at(z, x, y, 1 - k)
    ring = {o: (z + o) % NZ for o in range(1, NZ)}
    greet([up, down, east, west, far, other] + [at(ring[o], x, y, k) for o in range(1, NZ)])

    sent = []

    def go(src, dst, send, recv, device):
        copy = rcopy(src, dst, send, recv, device)
        copy.start()
        sent.append(copy)

    def came(dst, send, recv):
        rcopy(dst, dst, send, recv, other).wait_recv()

    def add(*values):
        total = values[0].astype(F32)
        for value in values[1:]:
            total = total + value.astype(F32)
        return total

    def columns(i):
        return grads.at[:, pl.ds(pl.multiple_of(i * COLS, COLS), COLS)]

    for i, (peer, device) in enumerate(((x2, far), (xp, east), (xm, west))):
        go(columns(peer), gx.at[x], gs.at[i], gr.at[i], device)
    own = pltpu.make_async_copy(columns(x), gx.at[x], loc.at[0])
    own.start()
    go(wg.at[:, 1 - k], w1, wcs, wcr, other)
    wload = pltpu.make_async_copy(wg.at[:, k], wa, loc.at[1])
    wload.start()

    place_row = lax.broadcasted_iota(jnp.int32, (128, 8 * SLOT), 0)

    def rows_of(q, core, out):
        residue = (z + OFFSETS[q] + NZ) % 4

        def body(i, carry):
            picked = rows[pl.ds(i * 4 + residue, 1), :] - core * 128
            hot = jnp.concatenate(
                [
                    jnp.where(picked - part * 256 == place_row, 1.0, 0.0).astype(BF)
                    for part in range(4)
                ],
                axis=0,
            )
            found = jnp.dot(
                hot, gx[...].reshape(8 * SLOT, COLS), preferred_element_type=F32
            ).astype(BF)
            out[q, i] = found.reshape(NY, 128, COLS)
            return carry

        lax.fori_loop(0, 4, body, 0)

    def compute(q):
        rows_of(q, 1 - k, to)
        go(to.at[q], t1.at[q], cs.at[q], cr.at[q], other)
        rows_of(q, k, ta)

    def t_core(q):
        came(t1.at[q], cs.at[q], cr.at[q])
        for i in range(4):
            ta[q, i] = add(ta[q, i], t1[q, i]).astype(BF)
        go(ta.at[q, :, y2, 0:64], tl1.at[q], ys.at[q, 0], yr.at[q, 0], up)
        go(ta.at[q, :, y2, 64:128], tr1.at[q], ys.at[q, 1], yr.at[q, 1], down)

    def t_y(q):
        came(tl1.at[q], ys.at[q, 0], yr.at[q, 0])
        ta[q, :, yp, 0:64] = add(ta[q, :, yp, 0:64], tl1[q]).astype(BF)
        go(ta.at[q, :, yp], tl2.at[q], ys.at[q, 2], yr.at[q, 2], up)
        came(tr1.at[q], ys.at[q, 1], yr.at[q, 1])
        ta[q, :, ym, 64:128] = add(ta[q, :, ym, 64:128], tr1[q]).astype(BF)
        go(ta.at[q, :, ym], tr2.at[q], ys.at[q, 3], yr.at[q, 3], down)

    def t_z(q):
        came(tl2.at[q], ys.at[q, 2], yr.at[q, 2])
        came(tr2.at[q], ys.at[q, 3], yr.at[q, 3])
        tb[q] = add(ta[q, :, y], tl2[q], tr2[q]).astype(BF)
        if q < 3:
            device = at((z + OFFSETS[q] + NZ) % NZ, x, y, k)
            go(tb.at[q], tz1.at[q], zs.at[q], zr.at[q], device)

    def t_z2():
        for q in range(3):
            came(tz1.at[q], zs.at[q], zr.at[q])
        ts[...] = add(tb[3], tz1[0], tz1[1], tz1[2]).astype(BF)
        for m in (2, 1, 3):
            zz = (z + 4 * m) % NZ
            go(ts.at[zz // 4], tz2.at[m - 1], z2s.at[m - 1], z2r.at[m - 1], at(zz, x, y, k))

    def t_end():
        total = ts[z // 4].astype(F32)
        for m in range(3):
            came(tz2.at[m], z2s.at[m], z2r.at[m])
            total = total + tz2[m].astype(F32)
        tout[...] = total * table_scale

    def w_core():
        wload.wait()
        came(w1, wcs, wcr)
        for i in range(4):
            wa[i] = add(wa[i], w1[i]).astype(BF)
        go(wa.at[0:2, x2], wl1, wxs.at[0], wxr.at[0], east)
        go(wa.at[2:4, x2], wr1, wxs.at[1], wxr.at[1], west)

    def w_x():
        came(wl1, wxs.at[0], wxr.at[0])
        wa[0:2, xp] = add(wa[0:2, xp], wl1[...]).astype(BF)
        go(wa.at[:, xp], wl2, wxs.at[2], wxr.at[2], east)
        came(wr1, wxs.at[1], wxr.at[1])
        wa[2:4, xm] = add(wa[2:4, xm], wr1[...]).astype(BF)
        go(wa.at[:, xm], wr2, wxs.at[3], wxr.at[3], west)

    def w_x2():
        came(wl2, wxs.at[2], wxr.at[2])
        came(wr2, wxs.at[3], wxr.at[3])
        wb[...] = add(wa[:, x], wl2[...], wr2[...]).astype(BF)
        go(wb.at[y2, :, 0:1280], vl1, wys.at[0], wyr.at[0], up)
        go(wb.at[y2, :, 1280:2560], vr1, wys.at[1], wyr.at[1], down)

    def w_y():
        came(vl1, wys.at[0], wyr.at[0])
        wb[yp, :, 0:1280] = add(wb[yp, :, 0:1280], vl1[...]).astype(BF)
        go(wb.at[yp], vl2, wys.at[2], wyr.at[2], up)
        came(vr1, wys.at[1], wyr.at[1])
        wb[ym, :, 1280:2560] = add(wb[ym, :, 1280:2560], vr1[...]).astype(BF)
        go(wb.at[ym], vr2, wys.at[3], wyr.at[3], down)

    def w_y2():
        came(vl2, wys.at[2], wyr.at[2])
        came(vr2, wys.at[3], wyr.at[3])
        summed = add(wb[y], vl2[...], vr2[...]).astype(BF)
        for j in range(NZ):
            wc[j, 0] = summed[:, j * 128:(j + 1) * 128]
            c = 16 + j // 4
            wc[j, 1] = summed[:, c * 128:(c + 1) * 128]
        for o in FAR_FIRST:
            zz = ring[o]
            go(wc.at[zz], wz.at[o - 1], wzs.at[o - 1], wzr.at[o - 1], at(zz, x, y, k))

    def w_z():
        total = wc[z].astype(F32)
        for o in range(1, NZ):
            came(wz.at[o - 1], wzs.at[o - 1], wzr.at[o - 1])
            total = total + wz[o - 1].astype(F32)
        wd[z] = total.astype(BF)
        for o in FAR_FIRST:
            go(wd.at[z], wd.at[z], wgs.at[o - 1], wgr.at[o - 1], at(ring[o], x, y, k))

    def w_z2():
        for o in range(1, NZ):
            came(wd.at[(z + NZ - o) % NZ], wgs.at[o - 1], wgr.at[o - 1])
        for j in range(16):
            we[x, :, j * 128:(j + 1) * 128] = wd[j, 0]
        for c in range(4):
            we[x, :, 2048 + c * 128:2048 + (c + 1) * 128] = wd[4 * c, 1]
        go(we.at[x], we.at[x], wes.at[0], wer.at[0], east)
        go(we.at[x], we.at[x], wes.at[1], wer.at[1], west)

    def w_x3():
        came(we.at[xm], wes.at[0], wer.at[0])
        part = we.at[xm, :, 0:1280]
        go(part, part, wes.at[2], wer.at[2], east)
        came(we.at[xp], wes.at[1], wer.at[1])
        part = we.at[xp, :, 1280:2560]
        go(part, part, wes.at[3], wer.at[3], west)

    def w_end():
        came(we.at[x2, :, 0:1280], wes.at[2], wer.at[2])
        came(we.at[x2, :, 1280:2560], wes.at[3], wer.at[3])
        for i in range(NX):
            total = we[i].astype(F32) * grad_scale
            win_out[i * 16:(i + 1) * 16, :] = total[:, :2048]
            wout_out[i * 16:(i + 1) * 16, :] = total[:, 2048:]

    own.wait()
    for i, source in enumerate((x2, xm, xp)):
        came(gx.at[source], gs.at[i], gr.at[i])
    compute(0)
    w_core()
    t_core(0)
    compute(1)
    w_x()
    t_y(0)
    t_core(1)
    compute(2)
    w_x2()
    t_z(0)
    t_y(1)
    t_core(2)
    compute(3)
    w_y()
    t_z(1)
    t_y(2)
    t_core(3)
    w_y2()
    t_z(2)
    t_y(3)
    w_z()
    t_z(3)
    t_z2()
    w_z2()
    w_x3()
    t_end()
    w_end()
    for copy in sent:
        copy.wait_send()


def back(grads, rows, wg, table_scale, grad_scale):
    v = pltpu.VMEM
    return pl.pallas_call(
        functools.partial(back_kernel, table_scale, grad_scale),
        name="back",
        out_shape=(
            jax.ShapeDtypeStruct((128, COLS), F32),
            jax.ShapeDtypeStruct((64, 2048), F32),
            jax.ShapeDtypeStruct((64, 512), F32),
        ),
        in_specs=[VM] * 3,
        out_specs=(VM,) * 3,
        scratch_shapes=[
            v((NX, 256, COLS), BF), v((4, 4, NY, 128, COLS), BF),
            v((4, 4, NY, 128, COLS), BF), v((4, 4, NY, 128, COLS), BF),
            v((4, 4, 64, COLS), BF), v((4, 4, 64, COLS), BF),
            v((4, 4, 128, COLS), BF), v((4, 4, 128, COLS), BF),
            v((4, 4, 128, COLS), BF), v((3, 4, 128, COLS), BF),
            v((4, 128, COLS), BF), v((3, 128, COLS), BF),
            v((NY, NX, 16, 2560), BF), v((NY, NX, 16, 2560), BF),
            v((2, 16, 2560), BF), v((2, 16, 2560), BF),
            v((4, 16, 2560), BF), v((4, 16, 2560), BF), v((4, 16, 2560), BF),
            v((16, 1280), BF), v((16, 1280), BF), v((16, 2560), BF), v((16, 2560), BF),
            v((NZ, 2, 16, 128), BF), v((15, 2, 16, 128), BF),
            v((NZ, 2, 16, 128), BF), v((NX, 16, 2560), BF),
            DMA((3,)), DMA((3,)),
            DMA((4,)), DMA((4,)), DMA((4, 4)), DMA((4, 4)), DMA((3,)), DMA((3,)),
            DMA((3,)), DMA((3,)), DMA((2,)),
            DMA, DMA, DMA((4,)), DMA((4,)), DMA((4,)), DMA((4,)),
            DMA((15,)), DMA((15,)), DMA((15,)), DMA((15,)), DMA((4,)), DMA((4,)),
        ],
        compiler_params=pltpu.CompilerParams(
            collective_id=3, has_side_effects=True, vmem_limit_bytes=VMEM_LIMIT
        ),
    )(grads, rows, wg)


def silu_grad(argument):
    logistic = jax.nn.sigmoid(argument)
    return logistic * (1.0 + argument * (1.0 - logistic))


def normalize(values):
    average = jnp.mean(values, axis=1, keepdims=True)
    centred = values - average
    inverse = lax.rsqrt(jnp.mean(centred * centred, axis=1, keepdims=True) + EPS)
    return centred * inverse, inverse


def norm_back(incoming, normed, inverse):
    first = jnp.mean(incoming, axis=1, keepdims=True)
    second = jnp.mean(incoming * normed, axis=1, keepdims=True)
    return inverse * (incoming - first - normed * second)


def dot(a, b, ca, cb):
    return lax.dot_general(a, b, (((ca,), (cb,)), ((), ())), preferred_element_type=F32)


def layer_kernel(lengths, rows, cot, w_in, w_out, out, grad, wg, act, proj, att, gh):
    width = D // HEADS
    scale = width ** (-0.5)
    values = rows[...].astype(F32)
    normed_in, in_inverse = normalize(values)
    half_in = normed_in.astype(BF)
    projected = dot(half_in, w_in[...], 1, 0)
    proj[...] = projected
    activated = jax.nn.silu(projected)
    gate = activated[:, :D]
    act[...] = activated[:, D:].astype(BF)
    place_i = lax.broadcasted_iota(jnp.int32, (SLOT, SLOT), 0)
    place_j = lax.broadcasted_iota(jnp.int32, (SLOT, SLOT), 1)
    masks = [
        (place_j <= place_i) & (place_i < lengths[s:s + 1, :]) for s in range(NSEQ)
    ]

    def heads(s, h):
        r = slice(s * SLOT, (s + 1) * SLOT)
        v = act[r, h * width:(h + 1) * width]
        q = act[r, D + h * width:D + (h + 1) * width]
        key = act[r, 2 * D + h * width:2 * D + (h + 1) * width]
        return r, v, q, key

    for s in range(NSEQ):
        for h in range(HEADS):
            r, v, q, key = heads(s, h)
            scores = dot(q, key, 1, 1) * scale
            weights = jnp.where(masks[s], jax.nn.silu(scores) * (1.0 / SLOT), 0.0).astype(BF)
            att[r, h * width:(h + 1) * width] = dot(weights, v, 1, 0)
    normed_out, out_inverse = normalize(att[...])
    mixed = (normed_out * gate).astype(BF)
    out[...] = (values + dot(mixed, w_out[...], 1, 0)).astype(BF)
    cotangent = cot[...]
    wg[:, 4 * D:] = dot(mixed, cotangent, 0, 0).astype(BF)
    grad_mixed = dot(cotangent, w_out[...], 1, 1)
    att[...] = norm_back(grad_mixed * gate, normed_out, out_inverse)
    gh[:, :D] = (grad_mixed * normed_out * silu_grad(proj[:, :D])).astype(BF)
    for s in range(NSEQ):
        for h in range(HEADS):
            r, v, q, key = heads(s, h)
            g = att[r, h * width:(h + 1) * width].astype(BF)
            scores = dot(q, key, 1, 1) * scale
            logistic = jax.nn.sigmoid(scores)
            weights = jnp.where(masks[s], scores * logistic * (1.0 / SLOT), 0.0).astype(BF)
            slope = logistic * (1.0 + scores * (1.0 - logistic))
            gw = dot(g, v, 1, 1)
            gs = jnp.where(masks[s], gw * (1.0 / SLOT) * slope, 0.0).astype(BF)
            parts = (
                dot(weights, g, 0, 0), dot(gs, key, 1, 0) * scale, dot(gs, q, 0, 0) * scale
            )
            for p in range(3):
                c = slice(D + p * D + h * width, D + p * D + (h + 1) * width)
                gh[r, c] = (parts[p] * silu_grad(proj[r, c])).astype(BF)
    grad_projected = gh[...]
    wg[:, :4 * D] = dot(half_in, grad_projected, 0, 0).astype(BF)
    grad_normed = dot(grad_projected, w_in[...], 1, 1)
    grad[...] = (
        cotangent.astype(F32) + norm_back(grad_normed, normed_in, in_inverse)
    ).astype(BF)


def layer(lengths, rows, cot, w_in, w_out):
    v = pltpu.VMEM
    return pl.pallas_call(
        layer_kernel,
        name="layer",
        out_shape=(
            jax.ShapeDtypeStruct((256, D), BF),
            jax.ShapeDtypeStruct((256, D), BF),
            jax.ShapeDtypeStruct((D, 5 * D), BF),
        ),
        in_specs=[VM] * 5,
        out_specs=(VM,) * 3,
        scratch_shapes=[
            v((256, 3 * D), BF), v((256, 4 * D), F32), v((256, D), F32), v((256, 4 * D), BF),
        ],
        compiler_params=pltpu.CompilerParams(vmem_limit_bytes=VMEM_LIMIT),
    )(lengths, rows, cot, w_in, w_out)


def on_device(
    item_ids, seq_lengths, surplus_slot, helper_map, embed_tables, weight_in, weight_out, cotangent
):
    z = lax.axis_index("emb") // NX
    near = lax.dynamic_slice_in_dim(item_ids[0], z * 1024, 1024, 0)
    ids = jnp.transpose(near.reshape(8, SLOT, TABLES), (0, 2, 1))
    meta = jnp.concatenate(
        [seq_lengths.reshape(16), surplus_slot.reshape(8), helper_map.reshape(8)]
    )
    meta = jnp.broadcast_to(meta[:, None], (32, 128))
    rows, id_rows, lengths, w_in, w_out = front(
        embed_tables.reshape(NY, 2, 128, COLS),
        weight_in.reshape(NX, 16, 2048),
        weight_out.reshape(NX, 16, 512),
        ids,
        meta,
    )
    forward_out, grad_rows, wg = layer(
        lengths, rows, cotangent[0], w_in.reshape(D, 4 * D), w_out.reshape(D, D)
    )
    events = NB * item_ids.shape[1]
    table_grad, grad_in, grad_out = back(
        grad_rows,
        id_rows,
        wg.reshape(NY, 2, NX, 16, 2560),
        (DISTINCT / events) ** 0.5,
        events ** (-0.5),
    )
    return forward_out[None], table_grad[None], grad_in, grad_out


def solution(mesh):
    placed = (
        P("bal", None, None),
        P(None, "emb", None),
        P(None, "emb"),
        P(None, "emb"),
        P("emb", None, None),
        P("bal", None),
        P("bal", None),
        P("bal", "emb", None),
    )
    return jax.shard_map(
        on_device,
        mesh=mesh,
        in_specs=placed,
        out_specs=(P("bal", "emb", None), P("emb", "bal", None), P("bal", None), P("bal", None)),
        check_vma=False,
    )
```

```python
import functools

import jax
import jax.numpy as jnp
from jax import lax
from jax.experimental import pallas as pl
from jax.experimental.pallas import tpu as pltpu
from jax.sharding import PartitionSpec as P

D = 512
HEADS = 8
COLS = 128
DISTINCT = 1024
SLOT = 128
NSEQ = 2
TABLES = 16
NZ = 16
NX = 4
NY = 4
NB = 8
EPS = 1e-05
BF = jnp.bfloat16
F32 = jnp.float32
VMEM_LIMIT = 64000 * 1024


def place():
    emb = lax.axis_index("emb")
    bal = lax.axis_index("bal")
    return emb // NX, emb % NX, bal // 2, bal % 2


def at(z, x, y, k):
    return {"emb": z * NX + x, "bal": y * 2 + k}


def rcopy(src, dst, send, recv, device):
    return pltpu.make_async_remote_copy(
        src_ref=src,
        dst_ref=dst,
        send_sem=send,
        recv_sem=recv,
        device_id=device,
        device_id_type=pl.DeviceIdType.MESH,
    )


def greet(devices):
    barrier = pltpu.get_barrier_semaphore()
    for device in devices:
        pl.semaphore_signal(barrier, inc=1, device_id=device, device_id_type=pl.DeviceIdType.MESH)
    pl.semaphore_wait(barrier, len(devices))


VM = pl.BlockSpec(memory_space=pltpu.VMEM)
ANY = pl.BlockSpec(memory_space=pl.ANY)
DMA = pltpu.SemaphoreType.DMA


ARRIVALS = (1, -1, 4, -4, 2, -2, 3, -3, 5, -5, 6, -6, 7, -7, 8)
INDEX = {offset: i for i, offset in enumerate(ARRIVALS)}
FIRST = (4, -4, 1, -1, 2, -2, 3, -3)
RELAYS = {4: (1, 2, 3, 4), -4: (-1, -2, -3)}


def front_kernel(
    tab, win, wout, ids, lengths, surpluses, helpers, out, id_rows, lens, wfi, wfo,
    tabs, idall, metall, columns, total, looked, meta,
    zs, zr, ys, yr, cs, cr, ws, wr, os_, or_, is_, ir, ms, mr, es, er, loc,
):
    z, x, y, k = place()
    bal = y * 2 + k
    y_peers = [(y + 1) % NY, (y + 3) % NY, (y + 2) % NY]
    x_peers = [(x + 1) % NX, (x + 3) % NX, (x + 2) % NX]
    y_from = [y_peers[1], y_peers[0], y_peers[2]]
    x_from = [x_peers[1], x_peers[0], x_peers[2]]
    y_devices = [at(z, x, peer, k) for peer in y_peers]
    x_devices = [at(z, peer, y, k) for peer in x_peers]
    other = at(z, x, y, 1 - k)
    z_devices = {o: at((z + o + NZ) % NZ, x, y, k) for o in FIRST}
    greet(list(z_devices.values()) + y_devices + x_devices + [other])

    sent = []

    def go(src, dst, send, recv, device):
        copy = rcopy(src, dst, send, recv, device)
        copy.start()
        sent.append(copy)

    def came(dst, send, recv):
        rcopy(dst, dst, send, recv, other).wait_recv()

    def origin(offset):
        return (z + NZ - offset) % NZ

    meta[0:8, :] = jnp.broadcast_to(lengths[:, 0:1], (NB, 128))
    meta[8:16, :] = jnp.broadcast_to(lengths[:, 1:2], (NB, 128))
    meta[16:24, :] = jnp.broadcast_to(surpluses[...], (NB, 128))
    meta[24:32, :] = jnp.broadcast_to(helpers[...], (NB, 128))
    for o in FIRST:
        i = INDEX[o]
        go(tab.at[y, k], tabs.at[z, y, k], zs.at[i], zr.at[i], z_devices[o])
    for i in range(3):
        go(ids, idall.at[y, k], is_.at[i], ir.at[i], y_devices[i])
        go(meta, metall.at[x], ms.at[i], mr.at[i], x_devices[i])
    for i in range(3):
        go(win.at[x], wfi.at[y, k, x], ws.at[i], wr.at[i], y_devices[i])
        go(wout.at[x], wfo.at[y, k, x], os_.at[i], or_.at[i], y_devices[i])
    local = [
        pltpu.make_async_copy(win.at[x], wfi.at[y, k, x], loc.at[0]),
        pltpu.make_async_copy(wout.at[x], wfo.at[y, k, x], loc.at[1]),
        pltpu.make_async_copy(ids, idall.at[y, k], loc.at[2]),
        pltpu.make_async_copy(meta, metall.at[x], loc.at[3]),
    ]
    for copy in local:
        copy.start()

    def from_z(pair):
        i, zz = INDEX[pair], origin(pair)
        mine = tabs.at[zz, y, k]
        came(mine, zs.at[i], zr.at[i])
        for r in RELAYS.get(pair, ()):
            j = INDEX[pair + r]
            go(mine, mine, zs.at[j], zr.at[j], z_devices[r])
        for p in range(3):
            go(mine, mine, ys.at[i, p], yr.at[i, p], y_devices[p])

    def from_y(pair):
        i, zz = INDEX[pair], origin(pair)
        for p in range(3):
            came(tabs.at[zz, y_from[p], k], ys.at[i, p], yr.at[i, p])
        go(tabs.at[zz, :, k], tabs.at[zz, :, k], cs.at[i], cr.at[i], other)

    def from_core(pair):
        i, zz = INDEX[pair], origin(pair)
        came(tabs.at[zz, :, 1 - k], cs.at[i], cr.at[i])

    lane = lax.broadcasted_iota(jnp.int32, (8 * SLOT, TABLES), 1)
    vocab = lax.broadcasted_iota(jnp.int32, (8 * SLOT, 256), 1)

    def sum_table(t, read):
        picked = jnp.sum(jnp.where(lane == t, columns[...], 0), axis=1, keepdims=True)

        def body(part, carry):
            hot = jnp.where(picked - part * 256 == vocab, 1.0, 0.0).astype(BF)
            total[...] += jnp.dot(hot, read(part), preferred_element_type=F32)
            return carry

        lax.fori_loop(0, 4, body, 0)

    def read_own(part):
        return tab[part].reshape(256, COLS)

    def choose_ids():
        for i in range(3):
            came(metall.at[x_from[i]], ms.at[i], mr.at[i])
        local[3].wait()
        came(idall.at[:, 1 - k], is_.at[3], ir.at[3])
        for xx in range(NX):
            mine = jnp.zeros((1, SLOT), jnp.int32)
            moved = jnp.zeros((TABLES, SLOT), jnp.int32)
            for b in range(NB):
                surplus = metall[xx, 16 + b:17 + b, :]
                is_mine = jnp.where(bal == b, 1, 0)
                mine = mine + surplus * is_mine
                sends = jnp.where(metall[xx, 24 + b:25 + b, :] == bal, 1, 0)
                first = idall[b // 2, b % 2, 2 * xx]
                second = idall[b // 2, b % 2, 2 * xx + 1]
                moved = moved + sends * (first + surplus * (second - first))
            for s in range(NSEQ):
                away = mine if s == 1 else 1 - mine
                kept = idall[y, k, 2 * xx + s]
                chosen = kept + away * (moved - kept)
                i = 2 * xx + s
                id_rows[:, i * SLOT:(i + 1) * SLOT] = chosen
                columns[i * SLOT:(i + 1) * SLOT, :] = jnp.transpose(chosen)
        mine = jnp.zeros((1, SLOT), jnp.int32)
        moved = jnp.zeros((1, SLOT), jnp.int32)
        kept = [jnp.zeros((1, SLOT), jnp.int32) for _ in range(NSEQ)]
        for b in range(NB):
            surplus = metall[x, 16 + b:17 + b, :]
            is_mine = jnp.where(bal == b, 1, 0)
            mine = mine + surplus * is_mine
            sends = jnp.where(metall[x, 24 + b:25 + b, :] == bal, 1, 0)
            first = metall[x, b:b + 1, :]
            second = metall[x, 8 + b:9 + b, :]
            moved = moved + sends * (first + surplus * (second - first))
            kept[0] = kept[0] + is_mine * first
            kept[1] = kept[1] + is_mine * second
        lens[...] = jnp.zeros_like(lens)
        lens[0:1, :] = kept[0] + (1 - mine) * (moved - kept[0])
        lens[1:2, :] = kept[1] + mine * (moved - kept[1])

    def ids_core():
        local[2].wait()
        for i in range(3):
            came(idall.at[y_from[i], k], is_.at[i], ir.at[i])
        go(idall.at[:, k], idall.at[:, k], is_.at[3], ir.at[3], other)

    def weights_x():
        local[0].wait()
        local[1].wait()
        for full, s_, r_ in ((wfi, ws, wr), (wfo, os_, or_)):
            for i in range(3):
                came(full.at[y_from[i], k, x], s_.at[i], r_.at[i])
            for i in range(3):
                part = full.at[:, k, x]
                go(part, part, s_.at[3 + i], r_.at[3 + i], x_devices[i])

    def weights_core():
        for full, s_, r_ in ((wfi, ws, wr), (wfo, os_, or_)):
            for i in range(3):
                came(full.at[:, k, x_from[i]], s_.at[3 + i], r_.at[3 + i])
            go(full.at[:, k], full.at[:, k], s_.at[6], r_.at[6], other)

    total[...] = jnp.zeros_like(total)
    for pair in ARRIVALS[:4]:
        from_z(pair)
    ids_core()
    for pair in ARRIVALS[4:8]:
        from_z(pair)
    from_y(ARRIVALS[0])
    choose_ids()
    sum_table(z, read_own)
    weights_x()
    for n in range(15):
        if n < 7:
            from_z(ARRIVALS[8 + n])
        if n < 14:
            from_y(ARRIVALS[n + 1])
        if n == 13:
            weights_core()
        from_core(ARRIVALS[n])
        zz = origin(ARRIVALS[n])
        sum_table(zz, lambda part, zz=zz: tabs[zz, part].reshape(256, COLS))

    looked[...] = total[...].astype(BF).reshape(NX, 256, COLS)

    def piece(i):
        return out.at[:, pl.ds(pl.multiple_of(i * COLS, COLS), COLS)]

    for i in (2, 0, 1):
        go(looked.at[x_peers[i]], piece(x), es.at[i], er.at[i], x_devices[i])
    own = pltpu.make_async_copy(looked.at[x], piece(x), loc.at[4])
    own.start()
    came(wfi.at[:, 1 - k], ws.at[6], wr.at[6])
    came(wfo.at[:, 1 - k], os_.at[6], or_.at[6])
    for i in range(3):
        came(piece(x_from[i]), es.at[i], er.at[i])
    own.wait()
    for copy in sent:
        copy.wait_send()


def front(tab, win, wout, ids, lengths, surpluses, helpers):
    v = pltpu.VMEM
    return pl.pallas_call(
        front_kernel,
        name="front",
        out_shape=(
            jax.ShapeDtypeStruct((256, D), BF),
            jax.ShapeDtypeStruct((TABLES, 8 * SLOT), jnp.int32),
            jax.ShapeDtypeStruct((8, SLOT), jnp.int32),
            jax.ShapeDtypeStruct((NY, 2, NX, 16, 2048), BF),
            jax.ShapeDtypeStruct((NY, 2, NX, 16, 512), BF),
        ),
        in_specs=[VM] * 7,
        out_specs=(VM, VM, VM, ANY, ANY),
        scratch_shapes=[
            v((NZ, NY, 2, 128, COLS), BF),
            v((NY, 2, 8, TABLES, SLOT), jnp.int32),
            v((NX, 32, 128), jnp.int32),
            v((8 * SLOT, TABLES), jnp.int32),
            v((8 * SLOT, COLS), F32),
            v((NX, 256, COLS), BF),
            v((32, 128), jnp.int32),
            DMA((15,)), DMA((15,)), DMA((15, 3)), DMA((15, 3)), DMA((15,)), DMA((15,)),
            DMA((7,)), DMA((7,)), DMA((7,)), DMA((7,)), DMA((4,)), DMA((4,)),
            DMA((3,)), DMA((3,)), DMA((3,)), DMA((3,)), DMA((5,)),
        ],
        compiler_params=pltpu.CompilerParams(
            collective_id=0, has_side_effects=True, vmem_limit_bytes=VMEM_LIMIT
        ),
    )(tab, win, wout, ids, lengths, surpluses, helpers)


def silu_grad(argument):
    logistic = jax.nn.sigmoid(argument)
    return logistic * (1.0 + argument * (1.0 - logistic))


def normalize(values):
    average = jnp.mean(values, axis=1, keepdims=True)
    centred = values - average
    inverse = lax.rsqrt(jnp.mean(centred * centred, axis=1, keepdims=True) + EPS)
    return centred * inverse, inverse


def norm_back(incoming, normed, inverse):
    first = jnp.mean(incoming, axis=1, keepdims=True)
    second = jnp.mean(incoming * normed, axis=1, keepdims=True)
    return inverse * (incoming - first - normed * second)


def dot(a, b, ca, cb):
    return lax.dot_general(a, b, (((ca,), (cb,)), ((), ())), preferred_element_type=F32)


def run_layer(lengths, rows, cot, w_in, w_out, out, grad, wg, act, proj, att, gh, wg_done):
    width = D // HEADS
    scale = width ** (-0.5)
    values = rows[...].astype(F32)
    normed_in, in_inverse = normalize(values)
    half_in = normed_in.astype(BF)
    projected = dot(half_in, w_in[...], 1, 0)
    proj[...] = projected
    activated = jax.nn.silu(projected)
    gate = activated[:, :D]
    act[...] = activated[:, D:].astype(BF)
    place_i = lax.broadcasted_iota(jnp.int32, (SLOT, SLOT), 0)
    place_j = lax.broadcasted_iota(jnp.int32, (SLOT, SLOT), 1)
    masks = [
        (place_j <= place_i) & (place_i < lengths[s:s + 1, :]) for s in range(NSEQ)
    ]

    def heads(s, h):
        r = slice(s * SLOT, (s + 1) * SLOT)
        v = act[r, h * width:(h + 1) * width]
        q = act[r, D + h * width:D + (h + 1) * width]
        key = act[r, 2 * D + h * width:2 * D + (h + 1) * width]
        return r, v, q, key

    for s in range(NSEQ):
        for h in range(HEADS):
            r, v, q, key = heads(s, h)
            scores = dot(q, key, 1, 1) * scale
            weights = jnp.where(masks[s], jax.nn.silu(scores) * (1.0 / SLOT), 0.0).astype(BF)
            att[r, h * width:(h + 1) * width] = dot(weights, v, 1, 0)
    normed_out, out_inverse = normalize(att[...])
    mixed = (normed_out * gate).astype(BF)
    out[...] = (values + dot(mixed, w_out[...], 1, 0)).astype(BF)
    cotangent = cot[...]
    wg[:, :, :, :, 4 * D:] = (
        dot(mixed, cotangent, 0, 0).astype(BF).reshape(NY, 2, NX, 16, D)
    )
    grad_mixed = dot(cotangent, w_out[...], 1, 1)
    att[...] = norm_back(grad_mixed * gate, normed_out, out_inverse)
    gh[:, :D] = (grad_mixed * normed_out * silu_grad(proj[:, :D])).astype(BF)
    for s in range(NSEQ):
        for h in range(HEADS):
            r, v, q, key = heads(s, h)
            g = att[r, h * width:(h + 1) * width].astype(BF)
            scores = dot(q, key, 1, 1) * scale
            logistic = jax.nn.sigmoid(scores)
            weights = jnp.where(masks[s], scores * logistic * (1.0 / SLOT), 0.0).astype(BF)
            slope = logistic * (1.0 + scores * (1.0 - logistic))
            gw = dot(g, v, 1, 1)
            gs = jnp.where(masks[s], gw * (1.0 / SLOT) * slope, 0.0).astype(BF)
            parts = (
                dot(weights, g, 0, 0), dot(gs, key, 1, 0) * scale, dot(gs, q, 0, 0) * scale
            )
            for p in range(3):
                c = slice(D + p * D + h * width, D + p * D + (h + 1) * width)
                gh[r, c] = (parts[p] * silu_grad(proj[r, c])).astype(BF)
    grad_projected = gh[...]
    wg[:, :, :, :, :4 * D] = (
        dot(half_in, grad_projected, 0, 0).astype(BF).reshape(NY, 2, NX, 16, 4 * D)
    )
    wg_done()
    grad_normed = dot(grad_projected, w_in[...], 1, 1)
    grad[...] = (
        cotangent.astype(F32) + norm_back(grad_normed, normed_in, in_inverse)
    ).astype(BF)


OFFSETS = (2, 1, -1, 0)
FAR_FIRST = (8, 7, 9, 6, 10, 5, 11, 4, 12, 3, 13, 2, 14, 1, 15)


def back_kernel(
    lengths, x_rows, cot, w_in, w_out, rows,
    layer_out, tout, we,
    grads, wg, act, proj, att, gh, gx, to, t1, ta, tl1, tr1, tl2, tr2, tb, tz1, ts, tz2,
    w1, wa, wp, wl1, wr1, wl, wr, wl2, wr2, wc, wz, wd,
    gs, gr, cs, cr, ys, yr, zs, zr, z2s, z2r, loc,
    wcs, wcr, wls, wlr, wrs, wrr, wzs, wzr, wgs, wgr, wes, wer,
):
    z, x, y, k = place()
    yp, ym, y2 = (y + 1) % NY, (y + 3) % NY, (y + 2) % NY
    xp, xm, x2 = (x + 1) % NX, (x + 3) % NX, (x + 2) % NX
    up, down = at(z, x, yp, k), at(z, x, ym, k)
    east, west, far = at(z, xp, y, k), at(z, xm, y, k), at(z, x2, y, k)
    other = at(z, x, y, 1 - k)
    x_peers, x_from, x_devices = (xp, xm, x2), (xm, xp, x2), (east, west, far)
    y_peers, y_devices = (yp, ym, y2), (up, down, at(z, x, y2, k))
    ring = {o: (z + o) % NZ for o in range(1, NZ)}
    greeted = [*y_devices, *x_devices, other] + [at(ring[o], x, y, k) for o in range(1, NZ)]
    barrier = pltpu.get_barrier_semaphore()
    for device in greeted:
        pl.semaphore_signal(barrier, inc=1, device_id=device, device_id_type=pl.DeviceIdType.MESH)

    sent = []

    def go(src, dst, send, recv, device):
        copy = rcopy(src, dst, send, recv, device)
        copy.start()
        sent.append(copy)

    def came(dst, send, recv):
        rcopy(dst, dst, send, recv, other).wait_recv()

    def add(*values):
        total = values[0].astype(F32)
        for value in values[1:]:
            total = total + value.astype(F32)
        return total

    chosen_sent = []

    def choose(condition, src, dst, send, recv, zz):
        both = rcopy(src, dst, send, recv, at(zz, x, y, k))
        one = rcopy(src.at[0], dst.at[0], send, recv, at(zz, x, y, k))

        @pl.when(condition)
        def _():
            both.start()

        @pl.when(jnp.logical_not(condition))
        def _():
            one.start()

        chosen_sent.append((condition, both, one))

    def chosen(condition, dst, send, recv):
        @pl.when(condition)
        def _():
            came(dst, send, recv)

        @pl.when(jnp.logical_not(condition))
        def _():
            came(dst.at[0], send, recv)

    def columns(i):
        return grads.at[:, pl.ds(pl.multiple_of(i * COLS, COLS), COLS)]

    def weights_ready():
        pl.semaphore_wait(barrier, len(greeted))
        go(wg.at[:, 1 - k], w1, wcs, wcr, other)

    run_layer(
        lengths, x_rows, cot, w_in, w_out, layer_out, grads, wg, act, proj, att, gh, weights_ready
    )

    for i, (peer, device) in enumerate(((x2, far), (xp, east), (xm, west))):
        go(columns(peer), gx.at[x], gs.at[i], gr.at[i], device)
    own = pltpu.make_async_copy(columns(x), gx.at[x], loc.at[0])
    own.start()

    place_row = lax.broadcasted_iota(jnp.int32, (128, 8 * SLOT), 0)

    def rows_of(q, core, out):
        residue = (z + OFFSETS[q] + NZ) % 4

        def body(i, carry):
            picked = rows[pl.ds(i * 4 + residue, 1), :] - core * 128
            hot = jnp.concatenate(
                [
                    jnp.where(picked - part * 256 == place_row, 1.0, 0.0).astype(BF)
                    for part in range(4)
                ],
                axis=0,
            )
            found = jnp.dot(
                hot, gx[...].reshape(8 * SLOT, COLS), preferred_element_type=F32
            ).astype(BF)
            out[q, i] = found.reshape(NY, 128, COLS)
            return carry

        lax.fori_loop(0, 4, body, 0)

    def compute(q):
        rows_of(q, 1 - k, to)
        go(to.at[q], t1.at[q], cs.at[q], cr.at[q], other)
        rows_of(q, k, ta)

    def t_core(q):
        came(t1.at[q], cs.at[q], cr.at[q])
        for i in range(4):
            ta[q, i] = add(ta[q, i], t1[q, i]).astype(BF)
        go(ta.at[q, :, y2, 0:64], tl1.at[q], ys.at[q, 0], yr.at[q, 0], up)
        go(ta.at[q, :, y2, 64:128], tr1.at[q], ys.at[q, 1], yr.at[q, 1], down)

    def t_y(q):
        came(tl1.at[q], ys.at[q, 0], yr.at[q, 0])
        ta[q, :, yp, 0:64] = add(ta[q, :, yp, 0:64], tl1[q]).astype(BF)
        go(ta.at[q, :, yp], tl2.at[q], ys.at[q, 2], yr.at[q, 2], up)
        came(tr1.at[q], ys.at[q, 1], yr.at[q, 1])
        ta[q, :, ym, 64:128] = add(ta[q, :, ym, 64:128], tr1[q]).astype(BF)
        go(ta.at[q, :, ym], tr2.at[q], ys.at[q, 3], yr.at[q, 3], down)

    def t_z(q):
        came(tl2.at[q], ys.at[q, 2], yr.at[q, 2])
        came(tr2.at[q], ys.at[q, 3], yr.at[q, 3])
        tb[q] = add(ta[q, :, y], tl2[q], tr2[q]).astype(BF)
        if q < 3:
            device = at((z + OFFSETS[q] + NZ) % NZ, x, y, k)
            go(tb.at[q], tz1.at[q], zs.at[q], zr.at[q], device)

    def t_z2():
        for q in range(3):
            came(tz1.at[q], zs.at[q], zr.at[q])
        ts[...] = add(tb[3], tz1[0], tz1[1], tz1[2]).astype(BF)
        for m in (2, 1, 3):
            zz = (z + 4 * m) % NZ
            go(ts.at[zz // 4], tz2.at[m - 1], z2s.at[m - 1], z2r.at[m - 1], at(zz, x, y, k))

    def t_end():
        total = ts[z // 4].astype(F32)
        for m in range(3):
            came(tz2.at[m], z2s.at[m], z2r.at[m])
            total = total + tz2[m].astype(F32)
        tout[...] = total

    def w_core():
        came(w1, wcs, wcr)
        for i in range(4):
            wa[i] = add(wg[i, k], w1[i]).astype(BF)
        for i in range(3):
            for j in range(NY):
                wp[i, j] = wa[j, x_peers[i], :, 0:1280]
        for i in range(3):
            go(wp.at[i], wl1.at[i], wls.at[0, i], wlr.at[0, i], x_devices[i])
            part = wa.at[y_peers[i], :, :, 1280:2560]
            go(part, wr1.at[i], wrs.at[0, i], wrr.at[0, i], y_devices[i])

    def w_first():
        for i in range(3):
            came(wl1.at[i], wls.at[0, i], wlr.at[0, i])
        wl[...] = add(wa[:, x, :, 0:1280], wl1[0], wl1[1], wl1[2]).astype(BF)
        for i in range(3):
            go(wl.at[y_peers[i]], wl2.at[i], wls.at[1, i], wlr.at[1, i], y_devices[i])
        for i in range(3):
            came(wr1.at[i], wrs.at[0, i], wrr.at[0, i])
        wr[...] = add(wa[y, :, :, 1280:2560], wr1[0], wr1[1], wr1[2]).astype(BF)
        for i in range(3):
            go(wr.at[x_peers[i]], wr2.at[i], wrs.at[1, i], wrr.at[1, i], x_devices[i])

    def w_second():
        for i in range(3):
            came(wl2.at[i], wls.at[1, i], wlr.at[1, i])
            came(wr2.at[i], wrs.at[1, i], wrr.at[1, i])
        low = add(wl[y], wl2[0], wl2[1], wl2[2]).astype(BF)
        high = add(wr[x], wr2[0], wr2[1], wr2[2]).astype(BF)
        tiles = [low[:, j * 128:(j + 1) * 128] for j in range(10)]
        tiles += [high[:, j * 128:(j + 1) * 128] for j in range(10)]
        for j in range(NZ):
            wc[j, 0] = tiles[j]
            wc[j, 1] = tiles[16 + j // 4]
        for o in FAR_FIRST:
            zz = ring[o]
            choose(zz % 4 == 0, wc.at[zz], wz.at[o - 1], wzs.at[o - 1], wzr.at[o - 1], zz)

    def w_z():
        for o in range(1, NZ):
            chosen(z % 4 == 0, wz.at[o - 1], wzs.at[o - 1], wzr.at[o - 1])
        total = wc[z].astype(F32)
        for o in range(1, NZ):
            total = total + wz[o - 1].astype(F32)
        wd[z] = total.astype(BF)
        for o in FAR_FIRST:
            choose(z % 4 == 0, wd.at[z], wd.at[z], wgs.at[o - 1], wgr.at[o - 1], ring[o])

    def w_z2():
        for o in range(1, NZ):
            zz = (z + NZ - o) % NZ
            chosen(zz % 4 == 0, wd.at[zz], wgs.at[o - 1], wgr.at[o - 1])
        for j in range(16):
            we[x, :, j * 128:(j + 1) * 128] = wd[j, 0]
        for c in range(4):
            we[x, :, 2048 + c * 128:2048 + (c + 1) * 128] = wd[4 * c, 1]
        for i in range(3):
            go(we.at[x], we.at[x], wes.at[i], wer.at[i], x_devices[i])

    def w_end():
        for i in range(3):
            came(we.at[x_from[i]], wes.at[i], wer.at[i])

    w_core()
    own.wait()
    for i, source in enumerate((x2, xm, xp)):
        came(gx.at[source], gs.at[i], gr.at[i])
    compute(0)
    t_core(0)
    compute(1)
    t_core(1)
    t_y(0)
    w_first()
    compute(2)
    t_core(2)
    t_y(1)
    t_z(0)
    w_second()
    compute(3)
    t_core(3)
    t_y(2)
    t_z(1)
    t_y(3)
    t_z(2)
    w_z()
    t_z(3)
    t_z2()
    w_z2()
    t_end()
    w_end()
    for copy in sent:
        copy.wait_send()
    for condition, both, one in chosen_sent:

        @pl.when(condition)
        def _():
            both.wait_send()

        @pl.when(jnp.logical_not(condition))
        def _():
            one.wait_send()


def back(lengths, x_rows, cot, w_in, w_out, rows):
    v = pltpu.VMEM
    return pl.pallas_call(
        back_kernel,
        name="back",
        out_shape=(
            jax.ShapeDtypeStruct((256, D), BF),
            jax.ShapeDtypeStruct((128, COLS), F32),
            jax.ShapeDtypeStruct((NX, 16, 2560), BF),
        ),
        in_specs=[VM] * 6,
        out_specs=(VM,) * 3,
        scratch_shapes=[
            v((256, D), BF), v((NY, 2, NX, 16, 2560), BF),
            v((256, 3 * D), BF), v((256, 4 * D), F32), v((256, D), F32), v((256, 4 * D), BF),
            v((NX, 256, COLS), BF), v((4, 4, NY, 128, COLS), BF),
            v((4, 4, NY, 128, COLS), BF), v((4, 4, NY, 128, COLS), BF),
            v((4, 4, 64, COLS), BF), v((4, 4, 64, COLS), BF),
            v((4, 4, 128, COLS), BF), v((4, 4, 128, COLS), BF),
            v((4, 4, 128, COLS), BF), v((3, 4, 128, COLS), BF),
            v((4, 128, COLS), BF), v((3, 128, COLS), BF),
            v((NY, NX, 16, 2560), BF), v((NY, NX, 16, 2560), BF),
            v((3, NY, 16, 1280), BF), v((3, NY, 16, 1280), BF), v((3, NX, 16, 1280), BF),
            v((NY, 16, 1280), BF), v((NX, 16, 1280), BF),
            v((3, 16, 1280), BF), v((3, 16, 1280), BF),
            v((NZ, 2, 16, 128), BF), v((15, 2, 16, 128), BF),
            v((NZ, 2, 16, 128), BF),
            DMA((3,)), DMA((3,)),
            DMA((4,)), DMA((4,)), DMA((4, 4)), DMA((4, 4)), DMA((3,)), DMA((3,)),
            DMA((3,)), DMA((3,)), DMA((2,)),
            DMA, DMA, DMA((2, 3)), DMA((2, 3)), DMA((2, 3)), DMA((2, 3)),
            DMA((15,)), DMA((15,)), DMA((15,)), DMA((15,)), DMA((3,)), DMA((3,)),
        ],
        compiler_params=pltpu.CompilerParams(
            collective_id=3, has_side_effects=True, vmem_limit_bytes=VMEM_LIMIT
        ),
    )(lengths, x_rows, cot, w_in, w_out, rows)


def finish_kernel(table_scale, grad_scale, layer_in, table_in, we, layer_out, table, gin, gout):
    layer_out[...] = layer_in[...]
    table[...] = table_in[...] * table_scale
    for i in range(NX):
        total = we[i].astype(F32) * grad_scale
        gin[i * 16:(i + 1) * 16, :] = total[:, :2048]
        gout[i * 16:(i + 1) * 16, :] = total[:, 2048:]


def finish(layer_out, table_sum, weight_sum, table_scale, grad_scale):
    return pl.pallas_call(
        functools.partial(finish_kernel, table_scale, grad_scale),
        name="finish",
        out_shape=(
            jax.ShapeDtypeStruct((256, D), BF),
            jax.ShapeDtypeStruct((128, COLS), F32),
            jax.ShapeDtypeStruct((64, 2048), F32),
            jax.ShapeDtypeStruct((64, 512), F32),
        ),
        in_specs=[VM] * 3,
        out_specs=(VM,) * 4,
    )(layer_out, table_sum, weight_sum)


def on_device(
    item_ids, seq_lengths, surplus_slot, helper_map, embed_tables, weight_in, weight_out, cotangent
):
    z = lax.axis_index("emb") // NX
    near = lax.dynamic_slice_in_dim(item_ids[0], z * 1024, 1024, 0)
    ids = jnp.transpose(near.reshape(8, SLOT, TABLES), (0, 2, 1))
    rows, id_rows, lengths, w_in, w_out = front(
        embed_tables.reshape(NY, 2, 128, COLS),
        weight_in.reshape(NX, 16, 2048),
        weight_out.reshape(NX, 16, 512),
        ids,
        seq_lengths.reshape(NB, NSEQ),
        surplus_slot,
        helper_map,
    )
    layer_out, table_sum, weight_sum = back(
        lengths, rows, cotangent[0], w_in.reshape(D, 4 * D), w_out.reshape(D, D), id_rows
    )
    events = NB * item_ids.shape[1]
    layer_out, table_grad, grad_in, grad_out = finish(
        layer_out, table_sum, weight_sum, (DISTINCT / events) ** 0.5, events ** (-0.5)
    )
    return layer_out[None], table_grad[None], grad_in, grad_out


def solution(mesh):
    placed = (
        P("bal", None, None),
        P(None, "emb", None),
        P(None, "emb"),
        P(None, "emb"),
        P("emb", None, None),
        P("bal", None),
        P("bal", None),
        P("bal", "emb", None),
    )
    return jax.shard_map(
        on_device,
        mesh=mesh,
        in_specs=placed,
        out_specs=(P("bal", "emb", None), P("emb", "bal", None), P("bal", None), P("bal", None)),
        check_vma=False,
    )
```

```python
import functools

import jax
import jax.numpy as jnp
from jax import lax
from jax.experimental import pallas as pl
from jax.experimental.pallas import tpu as pltpu
from jax.sharding import PartitionSpec as P

D = 512
HEADS = 8
COLS = 128
DISTINCT = 1024
SLOT = 128
NSEQ = 2
TABLES = 16
NZ = 16
NX = 4
NY = 4
NB = 8
EPS = 1e-05
BF = jnp.bfloat16
F32 = jnp.float32
VMEM_LIMIT = 64000 * 1024


def place():
    emb = lax.axis_index("emb")
    bal = lax.axis_index("bal")
    return emb // NX, emb % NX, bal // 2, bal % 2


def at(z, x, y, k):
    return {"emb": z * NX + x, "bal": y * 2 + k}


def rcopy(src, dst, send, recv, device):
    return pltpu.make_async_remote_copy(
        src_ref=src,
        dst_ref=dst,
        send_sem=send,
        recv_sem=recv,
        device_id=device,
        device_id_type=pl.DeviceIdType.MESH,
    )


def greet(devices):
    barrier = pltpu.get_barrier_semaphore()
    for device in devices:
        pl.semaphore_signal(barrier, inc=1, device_id=device, device_id_type=pl.DeviceIdType.MESH)
    pl.semaphore_wait(barrier, len(devices))


VM = pl.BlockSpec(memory_space=pltpu.VMEM)
ANY = pl.BlockSpec(memory_space=pl.ANY)
DMA = pltpu.SemaphoreType.DMA


ARRIVALS = (1, -1, 4, -4, 2, -2, 3, -3, 5, -5, 6, -6, 7, -7, 8)
INDEX = {offset: i for i, offset in enumerate(ARRIVALS)}
FIRST = (4, -4, 1, -1, 2, -2, 3, -3)
RELAYS = {4: (1, 2, 3, 4), -4: (-1, -2, -3)}


def front_kernel(
    tab, win, wout, ids, facts, out, id_rows, lens, wfi, wfo,
    tabs, idall, metall, columns, total, looked, meta,
    zs, zr, ys, yr, cs, cr, ws, wr, os_, or_, is_, ir, ms, mr, es, er, loc,
):
    z, x, y, k = place()
    bal = y * 2 + k
    y_peers = [(y + 1) % NY, (y + 3) % NY, (y + 2) % NY]
    x_peers = [(x + 1) % NX, (x + 3) % NX, (x + 2) % NX]
    y_from = [y_peers[1], y_peers[0], y_peers[2]]
    x_from = [x_peers[1], x_peers[0], x_peers[2]]
    y_devices = [at(z, x, peer, k) for peer in y_peers]
    x_devices = [at(z, peer, y, k) for peer in x_peers]
    other = at(z, x, y, 1 - k)
    z_devices = {o: at((z + o + NZ) % NZ, x, y, k) for o in FIRST}
    greet(list(z_devices.values()) + y_devices + x_devices + [other])

    sent = []

    def go(src, dst, send, recv, device):
        copy = rcopy(src, dst, send, recv, device)
        copy.start()
        sent.append(copy)

    def came(dst, send, recv):
        rcopy(dst, dst, send, recv, other).wait_recv()

    def origin(offset):
        return (z + NZ - offset) % NZ

    for i in range(4):
        meta[8 * i:8 * i + 8, :] = jnp.broadcast_to(facts[:, i:i + 1], (NB, 128))
    for o in FIRST:
        i = INDEX[o]
        go(tab.at[y, k], tabs.at[z, y, k], zs.at[i], zr.at[i], z_devices[o])
    for i in range(3):
        go(ids, idall.at[y, k], is_.at[i], ir.at[i], y_devices[i])
        go(meta, metall.at[x], ms.at[i], mr.at[i], x_devices[i])
    for i in range(3):
        go(win.at[x], wfi.at[y, k, x], ws.at[i], wr.at[i], y_devices[i])
        go(wout.at[x], wfo.at[y, k, x], os_.at[i], or_.at[i], y_devices[i])
    local = [
        pltpu.make_async_copy(win.at[x], wfi.at[y, k, x], loc.at[0]),
        pltpu.make_async_copy(wout.at[x], wfo.at[y, k, x], loc.at[1]),
        pltpu.make_async_copy(ids, idall.at[y, k], loc.at[2]),
        pltpu.make_async_copy(meta, metall.at[x], loc.at[3]),
    ]
    for copy in local:
        copy.start()

    def from_z(pair):
        i, zz = INDEX[pair], origin(pair)
        mine = tabs.at[zz, y, k]
        came(mine, zs.at[i], zr.at[i])
        for r in RELAYS.get(pair, ()):
            j = INDEX[pair + r]
            go(mine, mine, zs.at[j], zr.at[j], z_devices[r])
        for p in range(3):
            go(mine, mine, ys.at[i, p], yr.at[i, p], y_devices[p])

    def from_y(pair):
        i, zz = INDEX[pair], origin(pair)
        for p in range(3):
            came(tabs.at[zz, y_from[p], k], ys.at[i, p], yr.at[i, p])
        go(tabs.at[zz, :, k], tabs.at[zz, :, k], cs.at[i], cr.at[i], other)

    def from_core(pair):
        i, zz = INDEX[pair], origin(pair)
        came(tabs.at[zz, :, 1 - k], cs.at[i], cr.at[i])

    lane = lax.broadcasted_iota(jnp.int32, (8 * SLOT, TABLES), 1)
    vocab = lax.broadcasted_iota(jnp.int32, (8 * SLOT, 256), 1)

    def sum_table(t, read):
        picked = jnp.sum(jnp.where(lane == t, columns[...], 0), axis=1, keepdims=True)

        def body(part, carry):
            hot = jnp.where(picked - part * 256 == vocab, 1.0, 0.0).astype(BF)
            total[...] += jnp.dot(hot, read(part), preferred_element_type=F32)
            return carry

        lax.fori_loop(0, 4, body, 0)

    def read_own(part):
        return tab[part].reshape(256, COLS)

    def choose_ids():
        for i in range(3):
            came(metall.at[x_from[i]], ms.at[i], mr.at[i])
        local[3].wait()
        came(idall.at[:, 1 - k], is_.at[3], ir.at[3])
        for xx in range(NX):
            mine = jnp.zeros((1, SLOT), jnp.int32)
            moved = jnp.zeros((TABLES, SLOT), jnp.int32)
            for b in range(NB):
                surplus = metall[xx, 16 + b:17 + b, :]
                is_mine = jnp.where(bal == b, 1, 0)
                mine = mine + surplus * is_mine
                sends = jnp.where(metall[xx, 24 + b:25 + b, :] == bal, 1, 0)
                first = idall[b // 2, b % 2, 2 * xx]
                second = idall[b // 2, b % 2, 2 * xx + 1]
                moved = moved + sends * (first + surplus * (second - first))
            for s in range(NSEQ):
                away = mine if s == 1 else 1 - mine
                kept = idall[y, k, 2 * xx + s]
                chosen = kept + away * (moved - kept)
                i = 2 * xx + s
                id_rows[:, i * SLOT:(i + 1) * SLOT] = chosen
                columns[i * SLOT:(i + 1) * SLOT, :] = jnp.transpose(chosen)
        mine = jnp.zeros((1, SLOT), jnp.int32)
        moved = jnp.zeros((1, SLOT), jnp.int32)
        kept = [jnp.zeros((1, SLOT), jnp.int32) for _ in range(NSEQ)]
        for b in range(NB):
            surplus = metall[x, 16 + b:17 + b, :]
            is_mine = jnp.where(bal == b, 1, 0)
            mine = mine + surplus * is_mine
            sends = jnp.where(metall[x, 24 + b:25 + b, :] == bal, 1, 0)
            first = metall[x, b:b + 1, :]
            second = metall[x, 8 + b:9 + b, :]
            moved = moved + sends * (first + surplus * (second - first))
            kept[0] = kept[0] + is_mine * first
            kept[1] = kept[1] + is_mine * second
        lens[...] = jnp.zeros_like(lens)
        lens[0:1, :] = kept[0] + (1 - mine) * (moved - kept[0])
        lens[1:2, :] = kept[1] + mine * (moved - kept[1])

    def ids_core():
        local[2].wait()
        for i in range(3):
            came(idall.at[y_from[i], k], is_.at[i], ir.at[i])
        go(idall.at[:, k], idall.at[:, k], is_.at[3], ir.at[3], other)

    def weights_x():
        local[0].wait()
        local[1].wait()
        for full, s_, r_ in ((wfi, ws, wr), (wfo, os_, or_)):
            for i in range(3):
                came(full.at[y_from[i], k, x], s_.at[i], r_.at[i])
            for i in range(3):
                part = full.at[:, k, x]
                go(part, part, s_.at[3 + i], r_.at[3 + i], x_devices[i])

    def weights_core():
        for full, s_, r_ in ((wfi, ws, wr), (wfo, os_, or_)):
            for i in range(3):
                came(full.at[:, k, x_from[i]], s_.at[3 + i], r_.at[3 + i])
            go(full.at[:, k], full.at[:, k], s_.at[6], r_.at[6], other)

    total[...] = jnp.zeros_like(total)
    for pair in ARRIVALS[:4]:
        from_z(pair)
    ids_core()
    for pair in ARRIVALS[4:8]:
        from_z(pair)
    from_y(ARRIVALS[0])
    choose_ids()
    sum_table(z, read_own)
    weights_x()
    for n in range(15):
        if n < 7:
            from_z(ARRIVALS[8 + n])
        if n < 14:
            from_y(ARRIVALS[n + 1])
        if n == 13:
            weights_core()
        from_core(ARRIVALS[n])
        zz = origin(ARRIVALS[n])
        sum_table(zz, lambda part, zz=zz: tabs[zz, part].reshape(256, COLS))

    looked[...] = total[...].astype(BF).reshape(NX, 256, COLS)

    def piece(i):
        return out.at[:, pl.ds(pl.multiple_of(i * COLS, COLS), COLS)]

    for i in (2, 0, 1):
        go(looked.at[x_peers[i]], piece(x), es.at[i], er.at[i], x_devices[i])
    own = pltpu.make_async_copy(looked.at[x], piece(x), loc.at[4])
    own.start()
    came(wfi.at[:, 1 - k], ws.at[6], wr.at[6])
    came(wfo.at[:, 1 - k], os_.at[6], or_.at[6])
    for i in range(3):
        came(piece(x_from[i]), es.at[i], er.at[i])
    own.wait()
    for copy in sent:
        copy.wait_send()


def front(tab, win, wout, ids, facts):
    v = pltpu.VMEM
    return pl.pallas_call(
        front_kernel,
        name="front",
        out_shape=(
            jax.ShapeDtypeStruct((256, D), BF),
            jax.ShapeDtypeStruct((TABLES, 8 * SLOT), jnp.int32),
            jax.ShapeDtypeStruct((8, SLOT), jnp.int32),
            jax.ShapeDtypeStruct((NY, 2, NX, 16, 2048), BF),
            jax.ShapeDtypeStruct((NY, 2, NX, 16, 512), BF),
        ),
        in_specs=[VM] * 5,
        out_specs=(VM, VM, VM, ANY, ANY),
        scratch_shapes=[
            v((NZ, NY, 2, 128, COLS), BF),
            v((NY, 2, 8, TABLES, SLOT), jnp.int32),
            v((NX, 32, 128), jnp.int32),
            v((8 * SLOT, TABLES), jnp.int32),
            v((8 * SLOT, COLS), F32),
            v((NX, 256, COLS), BF),
            v((32, 128), jnp.int32),
            DMA((15,)), DMA((15,)), DMA((15, 3)), DMA((15, 3)), DMA((15,)), DMA((15,)),
            DMA((7,)), DMA((7,)), DMA((7,)), DMA((7,)), DMA((4,)), DMA((4,)),
            DMA((3,)), DMA((3,)), DMA((3,)), DMA((3,)), DMA((5,)),
        ],
        compiler_params=pltpu.CompilerParams(
            collective_id=0, has_side_effects=True, vmem_limit_bytes=VMEM_LIMIT
        ),
    )(tab, win, wout, ids, facts)


def silu_grad(argument):
    logistic = jax.nn.sigmoid(argument)
    return logistic * (1.0 + argument * (1.0 - logistic))


def normalize(values):
    average = jnp.mean(values, axis=1, keepdims=True)
    centred = values - average
    inverse = lax.rsqrt(jnp.mean(centred * centred, axis=1, keepdims=True) + EPS)
    return centred * inverse, inverse


def norm_back(incoming, normed, inverse):
    first = jnp.mean(incoming, axis=1, keepdims=True)
    second = jnp.mean(incoming * normed, axis=1, keepdims=True)
    return inverse * (incoming - first - normed * second)


def dot(a, b, ca, cb):
    return lax.dot_general(a, b, (((ca,), (cb,)), ((), ())), preferred_element_type=F32)


def run_layer(lengths, rows, cot, w_in, w_out, out, grad, wg, act, proj, att, gh, wg_done):
    width = D // HEADS
    scale = width ** (-0.5)
    values = rows[...].astype(F32)
    normed_in, in_inverse = normalize(values)
    half_in = normed_in.astype(BF)
    projected = dot(half_in, w_in[...], 1, 0)
    proj[...] = projected
    activated = jax.nn.silu(projected)
    gate = activated[:, :D]
    act[...] = activated[:, D:].astype(BF)
    place_i = lax.broadcasted_iota(jnp.int32, (SLOT, SLOT), 0)
    place_j = lax.broadcasted_iota(jnp.int32, (SLOT, SLOT), 1)
    masks = [
        (place_j <= place_i) & (place_i < lengths[s:s + 1, :]) for s in range(NSEQ)
    ]

    def heads(s, h):
        r = slice(s * SLOT, (s + 1) * SLOT)
        v = act[r, h * width:(h + 1) * width]
        q = act[r, D + h * width:D + (h + 1) * width]
        key = act[r, 2 * D + h * width:2 * D + (h + 1) * width]
        return r, v, q, key

    for s in range(NSEQ):
        for h in range(HEADS):
            r, v, q, key = heads(s, h)
            scores = dot(q, key, 1, 1) * scale
            weights = jnp.where(masks[s], jax.nn.silu(scores) * (1.0 / SLOT), 0.0).astype(BF)
            att[r, h * width:(h + 1) * width] = dot(weights, v, 1, 0)
    normed_out, out_inverse = normalize(att[...])
    mixed = (normed_out * gate).astype(BF)
    out[...] = (values + dot(mixed, w_out[...], 1, 0)).astype(BF)
    cotangent = cot[...]
    wg[:, :, :, :, 4 * D:] = (
        dot(mixed, cotangent, 0, 0).astype(BF).reshape(NY, 2, NX, 16, D)
    )
    grad_mixed = dot(cotangent, w_out[...], 1, 1)
    att[...] = norm_back(grad_mixed * gate, normed_out, out_inverse)
    gh[:, :D] = (grad_mixed * normed_out * silu_grad(proj[:, :D])).astype(BF)
    for s in range(NSEQ):
        for h in range(HEADS):
            r, v, q, key = heads(s, h)
            g = att[r, h * width:(h + 1) * width].astype(BF)
            scores = dot(q, key, 1, 1) * scale
            logistic = jax.nn.sigmoid(scores)
            weights = jnp.where(masks[s], scores * logistic * (1.0 / SLOT), 0.0).astype(BF)
            slope = logistic * (1.0 + scores * (1.0 - logistic))
            gw = dot(g, v, 1, 1)
            gs = jnp.where(masks[s], gw * (1.0 / SLOT) * slope, 0.0).astype(BF)
            parts = (
                dot(weights, g, 0, 0), dot(gs, key, 1, 0) * scale, dot(gs, q, 0, 0) * scale
            )
            for p in range(3):
                c = slice(D + p * D + h * width, D + p * D + (h + 1) * width)
                gh[r, c] = (parts[p] * silu_grad(proj[r, c])).astype(BF)
    grad_projected = gh[...]
    wg[:, :, :, :, :4 * D] = (
        dot(half_in, grad_projected, 0, 0).astype(BF).reshape(NY, 2, NX, 16, 4 * D)
    )
    wg_done()
    grad_normed = dot(grad_projected, w_in[...], 1, 1)
    grad[...] = (
        cotangent.astype(F32) + norm_back(grad_normed, normed_in, in_inverse)
    ).astype(BF)


OFFSETS = (2, 1, -1, 0)
FAR_FIRST = (8, 7, 9, 6, 10, 5, 11, 4, 12, 3, 13, 2, 14, 1, 15)


def back_kernel(
    lengths, x_rows, cot, w_in, w_out, rows,
    layer_out, tout, we,
    grads, wg, act, proj, att, gh, gx, to, t1, ta, tl1, tr1, tl2, tr2, tb, tz1, ts, tz2,
    w1, wa, wp, wl1, wr1, wl, wr, wl2, wr2, wc, wz, wd,
    gs, gr, cs, cr, ys, yr, zs, zr, z2s, z2r, loc,
    wcs, wcr, wls, wlr, wrs, wrr, wzs, wzr, wgs, wgr, wes, wer,
):
    z, x, y, k = place()
    yp, ym, y2 = (y + 1) % NY, (y + 3) % NY, (y + 2) % NY
    xp, xm, x2 = (x + 1) % NX, (x + 3) % NX, (x + 2) % NX
    up, down = at(z, x, yp, k), at(z, x, ym, k)
    east, west, far = at(z, xp, y, k), at(z, xm, y, k), at(z, x2, y, k)
    other = at(z, x, y, 1 - k)
    x_peers, x_from, x_devices = (xp, xm, x2), (xm, xp, x2), (east, west, far)
    y_peers, y_devices = (yp, ym, y2), (up, down, at(z, x, y2, k))
    ring = {o: (z + o) % NZ for o in range(1, NZ)}
    greeted = [*y_devices, *x_devices, other] + [at(ring[o], x, y, k) for o in range(1, NZ)]
    barrier = pltpu.get_barrier_semaphore()
    for device in greeted:
        pl.semaphore_signal(barrier, inc=1, device_id=device, device_id_type=pl.DeviceIdType.MESH)

    sent = []

    def go(src, dst, send, recv, device):
        copy = rcopy(src, dst, send, recv, device)
        copy.start()
        sent.append(copy)

    def came(dst, send, recv):
        rcopy(dst, dst, send, recv, other).wait_recv()

    def add(*values):
        total = values[0].astype(F32)
        for value in values[1:]:
            total = total + value.astype(F32)
        return total

    chosen_sent = []

    def choose(condition, src, dst, send, recv, zz):
        both = rcopy(src, dst, send, recv, at(zz, x, y, k))
        one = rcopy(src.at[0], dst.at[0], send, recv, at(zz, x, y, k))

        @pl.when(condition)
        def _():
            both.start()

        @pl.when(jnp.logical_not(condition))
        def _():
            one.start()

        chosen_sent.append((condition, both, one))

    def chosen(condition, dst, send, recv):
        @pl.when(condition)
        def _():
            came(dst, send, recv)

        @pl.when(jnp.logical_not(condition))
        def _():
            came(dst.at[0], send, recv)

    def columns(i):
        return grads.at[:, pl.ds(pl.multiple_of(i * COLS, COLS), COLS)]

    def weights_ready():
        pl.semaphore_wait(barrier, len(greeted))
        go(wg.at[:, 1 - k], w1, wcs, wcr, other)

    run_layer(
        lengths, x_rows, cot, w_in, w_out, layer_out, grads, wg, act, proj, att, gh, weights_ready
    )

    for i, (peer, device) in enumerate(((x2, far), (xp, east), (xm, west))):
        go(columns(peer), gx.at[x], gs.at[i], gr.at[i], device)
    own = pltpu.make_async_copy(columns(x), gx.at[x], loc.at[0])
    own.start()

    place_row = lax.broadcasted_iota(jnp.int32, (128, 8 * SLOT), 0)

    def rows_of(q, core, out):
        residue = (z + OFFSETS[q] + NZ) % 4

        def body(i, carry):
            picked = rows[pl.ds(i * 4 + residue, 1), :] - core * 128
            hot = jnp.concatenate(
                [
                    jnp.where(picked - part * 256 == place_row, 1.0, 0.0).astype(BF)
                    for part in range(4)
                ],
                axis=0,
            )
            found = jnp.dot(
                hot, gx[...].reshape(8 * SLOT, COLS), preferred_element_type=F32
            ).astype(BF)
            out[q, i] = found.reshape(NY, 128, COLS)
            return carry

        lax.fori_loop(0, 4, body, 0)

    def compute(q):
        rows_of(q, 1 - k, to)
        go(to.at[q], t1.at[q], cs.at[q], cr.at[q], other)
        rows_of(q, k, ta)

    def t_core(q):
        came(t1.at[q], cs.at[q], cr.at[q])
        for i in range(4):
            ta[q, i] = add(ta[q, i], t1[q, i]).astype(BF)
        go(ta.at[q, :, y2, 0:64], tl1.at[q], ys.at[q, 0], yr.at[q, 0], up)
        go(ta.at[q, :, y2, 64:128], tr1.at[q], ys.at[q, 1], yr.at[q, 1], down)

    def t_y(q):
        came(tl1.at[q], ys.at[q, 0], yr.at[q, 0])
        ta[q, :, yp, 0:64] = add(ta[q, :, yp, 0:64], tl1[q]).astype(BF)
        go(ta.at[q, :, yp], tl2.at[q], ys.at[q, 2], yr.at[q, 2], up)
        came(tr1.at[q], ys.at[q, 1], yr.at[q, 1])
        ta[q, :, ym, 64:128] = add(ta[q, :, ym, 64:128], tr1[q]).astype(BF)
        go(ta.at[q, :, ym], tr2.at[q], ys.at[q, 3], yr.at[q, 3], down)

    def t_z(q):
        came(tl2.at[q], ys.at[q, 2], yr.at[q, 2])
        came(tr2.at[q], ys.at[q, 3], yr.at[q, 3])
        tb[q] = add(ta[q, :, y], tl2[q], tr2[q]).astype(BF)
        if q < 3:
            device = at((z + OFFSETS[q] + NZ) % NZ, x, y, k)
            go(tb.at[q], tz1.at[q], zs.at[q], zr.at[q], device)

    def t_z2():
        for q in range(3):
            came(tz1.at[q], zs.at[q], zr.at[q])
        ts[...] = add(tb[3], tz1[0], tz1[1], tz1[2]).astype(BF)
        for m in (2, 1, 3):
            zz = (z + 4 * m) % NZ
            go(ts.at[zz // 4], tz2.at[m - 1], z2s.at[m - 1], z2r.at[m - 1], at(zz, x, y, k))

    def t_end():
        total = ts[z // 4].astype(F32)
        for m in range(3):
            came(tz2.at[m], z2s.at[m], z2r.at[m])
            total = total + tz2[m].astype(F32)
        tout[...] = total

    def w_core():
        came(w1, wcs, wcr)
        for i in range(4):
            wa[i] = add(wg[i, k], w1[i]).astype(BF)
        for i in range(3):
            for j in range(NY):
                wp[i, j] = wa[j, x_peers[i], :, 0:1280]
        for i in range(3):
            go(wp.at[i], wl1.at[i], wls.at[0, i], wlr.at[0, i], x_devices[i])
            part = wa.at[y_peers[i], :, :, 1280:2560]
            go(part, wr1.at[i], wrs.at[0, i], wrr.at[0, i], y_devices[i])

    def w_first():
        for i in range(3):
            came(wl1.at[i], wls.at[0, i], wlr.at[0, i])
        wl[...] = add(wa[:, x, :, 0:1280], wl1[0], wl1[1], wl1[2]).astype(BF)
        for i in range(3):
            go(wl.at[y_peers[i]], wl2.at[i], wls.at[1, i], wlr.at[1, i], y_devices[i])
        for i in range(3):
            came(wr1.at[i], wrs.at[0, i], wrr.at[0, i])
        wr[...] = add(wa[y, :, :, 1280:2560], wr1[0], wr1[1], wr1[2]).astype(BF)
        for i in range(3):
            go(wr.at[x_peers[i]], wr2.at[i], wrs.at[1, i], wrr.at[1, i], x_devices[i])

    def w_second():
        for i in range(3):
            came(wl2.at[i], wls.at[1, i], wlr.at[1, i])
            came(wr2.at[i], wrs.at[1, i], wrr.at[1, i])
        low = add(wl[y], wl2[0], wl2[1], wl2[2]).astype(BF)
        high = add(wr[x], wr2[0], wr2[1], wr2[2]).astype(BF)
        tiles = [low[:, j * 128:(j + 1) * 128] for j in range(10)]
        tiles += [high[:, j * 128:(j + 1) * 128] for j in range(10)]
        for j in range(NZ):
            wc[j, 0] = tiles[j]
            wc[j, 1] = tiles[16 + j // 4]
        for o in FAR_FIRST:
            zz = ring[o]
            choose(zz % 4 == 0, wc.at[zz], wz.at[o - 1], wzs.at[o - 1], wzr.at[o - 1], zz)

    def w_z():
        for o in range(1, NZ):
            chosen(z % 4 == 0, wz.at[o - 1], wzs.at[o - 1], wzr.at[o - 1])
        total = wc[z].astype(F32)
        for o in range(1, NZ):
            total = total + wz[o - 1].astype(F32)
        wd[z] = total.astype(BF)
        for o in FAR_FIRST:
            choose(z % 4 == 0, wd.at[z], wd.at[z], wgs.at[o - 1], wgr.at[o - 1], ring[o])

    def w_z2():
        for o in range(1, NZ):
            zz = (z + NZ - o) % NZ
            chosen(zz % 4 == 0, wd.at[zz], wgs.at[o - 1], wgr.at[o - 1])
        for j in range(16):
            we[x, :, j * 128:(j + 1) * 128] = wd[j, 0]
        for c in range(4):
            we[x, :, 2048 + c * 128:2048 + (c + 1) * 128] = wd[4 * c, 1]
        for i in range(3):
            go(we.at[x], we.at[x], wes.at[i], wer.at[i], x_devices[i])

    def w_end():
        for i in range(3):
            came(we.at[x_from[i]], wes.at[i], wer.at[i])

    w_core()
    own.wait()
    for i, source in enumerate((x2, xm, xp)):
        came(gx.at[source], gs.at[i], gr.at[i])
    compute(0)
    t_core(0)
    compute(1)
    t_core(1)
    t_y(0)
    w_first()
    compute(2)
    t_core(2)
    t_y(1)
    t_z(0)
    w_second()
    compute(3)
    t_core(3)
    t_y(2)
    t_z(1)
    t_y(3)
    t_z(2)
    w_z()
    t_z(3)
    t_z2()
    w_z2()
    t_end()
    w_end()
    for copy in sent:
        copy.wait_send()
    for condition, both, one in chosen_sent:

        @pl.when(condition)
        def _():
            both.wait_send()

        @pl.when(jnp.logical_not(condition))
        def _():
            one.wait_send()


def back(lengths, x_rows, cot, w_in, w_out, rows):
    v = pltpu.VMEM
    return pl.pallas_call(
        back_kernel,
        name="back",
        out_shape=(
            jax.ShapeDtypeStruct((256, D), BF),
            jax.ShapeDtypeStruct((128, COLS), F32),
            jax.ShapeDtypeStruct((NX, 16, 2560), BF),
        ),
        in_specs=[VM] * 6,
        out_specs=(VM,) * 3,
        scratch_shapes=[
            v((256, D), BF), v((NY, 2, NX, 16, 2560), BF),
            v((256, 3 * D), BF), v((256, 4 * D), F32), v((256, D), F32), v((256, 4 * D), BF),
            v((NX, 256, COLS), BF), v((4, 4, NY, 128, COLS), BF),
            v((4, 4, NY, 128, COLS), BF), v((4, 4, NY, 128, COLS), BF),
            v((4, 4, 64, COLS), BF), v((4, 4, 64, COLS), BF),
            v((4, 4, 128, COLS), BF), v((4, 4, 128, COLS), BF),
            v((4, 4, 128, COLS), BF), v((3, 4, 128, COLS), BF),
            v((4, 128, COLS), BF), v((3, 128, COLS), BF),
            v((NY, NX, 16, 2560), BF), v((NY, NX, 16, 2560), BF),
            v((3, NY, 16, 1280), BF), v((3, NY, 16, 1280), BF), v((3, NX, 16, 1280), BF),
            v((NY, 16, 1280), BF), v((NX, 16, 1280), BF),
            v((3, 16, 1280), BF), v((3, 16, 1280), BF),
            v((NZ, 2, 16, 128), BF), v((15, 2, 16, 128), BF),
            v((NZ, 2, 16, 128), BF),
            DMA((3,)), DMA((3,)),
            DMA((4,)), DMA((4,)), DMA((4, 4)), DMA((4, 4)), DMA((3,)), DMA((3,)),
            DMA((3,)), DMA((3,)), DMA((2,)),
            DMA, DMA, DMA((2, 3)), DMA((2, 3)), DMA((2, 3)), DMA((2, 3)),
            DMA((15,)), DMA((15,)), DMA((15,)), DMA((15,)), DMA((3,)), DMA((3,)),
        ],
        compiler_params=pltpu.CompilerParams(
            collective_id=3, has_side_effects=True, vmem_limit_bytes=VMEM_LIMIT
        ),
    )(lengths, x_rows, cot, w_in, w_out, rows)


def finish_kernel(table_scale, grad_scale, layer_in, table_in, we, layer_out, table, gin, gout):
    layer_out[...] = layer_in[...]
    table[...] = table_in[...] * table_scale
    for i in range(NX):
        total = we[i].astype(F32) * grad_scale
        gin[i * 16:(i + 1) * 16, :] = total[:, :2048]
        gout[i * 16:(i + 1) * 16, :] = total[:, 2048:]


def finish(layer_out, table_sum, weight_sum, table_scale, grad_scale):
    return pl.pallas_call(
        functools.partial(finish_kernel, table_scale, grad_scale),
        name="finish",
        out_shape=(
            jax.ShapeDtypeStruct((256, D), BF),
            jax.ShapeDtypeStruct((128, COLS), F32),
            jax.ShapeDtypeStruct((64, 2048), F32),
            jax.ShapeDtypeStruct((64, 512), F32),
        ),
        in_specs=[VM] * 3,
        out_specs=(VM,) * 4,
    )(layer_out, table_sum, weight_sum)


def on_device(
    item_ids, seq_lengths, surplus_slot, helper_map, embed_tables, weight_in, weight_out, cotangent
):
    z = lax.axis_index("emb") // NX
    near = lax.dynamic_slice_in_dim(item_ids[0], z * 1024, 1024, 0)
    ids = jnp.transpose(near.reshape(8, SLOT, TABLES), (0, 2, 1))
    rows, id_rows, lengths, w_in, w_out = front(
        embed_tables.reshape(NY, 2, 128, COLS),
        weight_in.reshape(NX, 16, 2048),
        weight_out.reshape(NX, 16, 512),
        ids,
        jnp.concatenate([seq_lengths[:, 0, :], surplus_slot, helper_map], axis=1),
    )
    layer_out, table_sum, weight_sum = back(
        lengths, rows, cotangent[0], w_in.reshape(D, 4 * D), w_out.reshape(D, D), id_rows
    )
    events = NB * item_ids.shape[1]
    layer_out, table_grad, grad_in, grad_out = finish(
        layer_out, table_sum, weight_sum, (DISTINCT / events) ** 0.5, events ** (-0.5)
    )
    return layer_out[None], table_grad[None], grad_in, grad_out


def solution(mesh):
    placed = (
        P("bal", None, None),
        P(None, "emb", None),
        P(None, "emb"),
        P(None, "emb"),
        P("emb", None, None),
        P("bal", None),
        P("bal", None),
        P("bal", "emb", None),
    )
    return jax.shard_map(
        on_device,
        mesh=mesh,
        in_specs=placed,
        out_specs=(P("bal", "emb", None), P("emb", "bal", None), P("bal", None), P("bal", None)),
        check_vma=False,
    )
```
